32 devices in a mesh: mode: 2 (over x), space: 16 (over z, y, core).
Axes of the slice: x: 2, y: 2, z: 4, core: 2. Of those that a mesh axis runs over, the one named last changes fastest.
Arguments:
- field: bfloat16 [64, 256, 1024], P('mode', 'space'), may hold values from -6 to 6
- kappa_x: float32 [8, 256, 1024], P(None, 'space'), may hold values from -4 to 4
- kappa_y: float32 [8, 256, 1024], P(None, 'space'), may hold values from -4 to 4
- coupling: bfloat16 [4, 8, 32, 32], P('mode'), may hold values from -0.625 to 0.625
- pattern: int32 [4, 8, 32, 32], P('mode'), may hold values 0 or 1
Outputs:
- image: float32 [64, 256, 1024], P('mode', 'space')
The draws below stay inside these ranges and needn't reach their ends.
All inputs are finite; a program needn't handle non-finite values. No bound on the sum of `pattern` on one device may be relied on, other than what follows from the above.
Results may differ from the reference program's by a relative error of at most 0.0003.
Values may be sent and summed in bfloat16 or wider, within the bound.
A program may use at most 64 MiB of HBM per device.

```python
import jax
import jax.numpy as jnp
from jax import lax

MB = 32
K = 8
ROUNDS = 1
NY = 1024
MODES = 64
NX = 256
N_MODE = 2


def place_ends(values, rng, least, high):
    place = [jax.random.randint(jax.random.fold_in(rng, axis), (), 0, length) for axis, length in enumerate(values.shape)]
    main_axis = values.shape.index(max(values.shape))
    beside = place[:main_axis] + [(place[main_axis] + 1) % values.shape[main_axis]] + place[main_axis + 1:]
    return values.at[tuple(place)].set(least).at[tuple(beside)].set(high)


def shard_levels(stream_key, dims, pieces, low, high):
    gain = 1.0
    for axis_at, shards_of in pieces:
        steps = jax.random.uniform(jax.random.fold_in(jax.random.fold_in(stream_key, 6), axis_at), (shards_of,), jnp.float32, low / len(pieces), high / len(pieces))
        gain = gain * jnp.repeat(jnp.exp(steps), dims[axis_at] // shards_of).reshape((-1,) + (1,) * (len(dims) - 1 - axis_at))
    return gain


def gaussian(rng, extent, deviation, limit, shards=(), kind=jnp.bfloat16):
    level = shard_levels(rng, extent, shards, -0.22, 0.18) if shards else 1.0
    values = jax.random.normal(rng, extent, jnp.float32) * deviation * level
    return jnp.minimum(jnp.maximum(values, -limit), limit).astype(kind)


def setup_inputs(seed: int = 0) -> dict:
    seeds = jax.random.split(jax.random.key(seed), 6)
    return {
        "field": gaussian(seeds[0], (MODES, NX, NY), 1.0, 6.0, ((0, 2), (1, 16))),
        "kappa_x": gaussian(seeds[1], (K, NX, NY), 0.5, 4.0, ((1, 16),), jnp.float32),
        "kappa_y": gaussian(seeds[2], (K, NX, NY), 0.5, 4.0, ((1, 16),), jnp.float32),
        "coupling": gaussian(seeds[3], (N_MODE * (ROUNDS + 1), K, MB, MB), (3 * MB) ** -0.5, 0.625, ((0, 2),)),
        "pattern": place_ends((jax.random.randint(seeds[4], (N_MODE * (ROUNDS + 1), K, MB, MB), 0, 3) < 1).astype(jnp.int32), jax.random.fold_in(seeds[4], 1), 0, 1),
    }


def mix(coef_k, block):
    return jnp.einsum("ij,jrw->irw", coef_k, block, precision=lax.Precision.HIGHEST)


def reference(field, kappa_x, kappa_y, coupling, pattern):
    zeros_bf = jnp.zeros(coupling.shape, jnp.bfloat16)
    coef = jnp.where(pattern > 0, coupling, zeros_bf).astype(jnp.float32)
    coef = coef.reshape(N_MODE, ROUNDS + 1, K, MB, MB)
    blocks = field.astype(jnp.float32).reshape(N_MODE, MB, NX, NY)
    padded = jnp.concatenate([blocks, jnp.zeros((N_MODE, MB, 1, NY), jnp.float32)], axis=2)

    def one_block(index):
        own = padded[index]
        flux_x = jnp.zeros((MB, NX, NY), jnp.float32)
        flux_y = jnp.zeros((MB, NX, NY), jnp.float32)
        for k in range(K):
            ck = coef[index, 0, k]
            wk = 0.5 * (mix(ck, own) + mix(ck.T, own))
            for r in range(1, ROUNDS + 1):
                upper = (index + r) % N_MODE
                lower = (index - r) % N_MODE
                wk = wk + mix(coef[index, r, k], padded[upper]) + mix(coef[lower, r, k].T, padded[lower])
            inner = wk[:, :NX, :]
            diff_x = wk[:, 1:, :] - inner
            next_col = jnp.concatenate([inner[:, :, 1:], jnp.zeros((MB, NX, 1), jnp.float32)], axis=2)
            flux_x = flux_x + kappa_x[k] * diff_x
            flux_y = flux_y + kappa_y[k] * (next_col - inner)
        prev_x = jnp.concatenate([jnp.zeros((MB, 1, NY), jnp.float32), flux_x[:, :-1, :]], axis=1)
        prev_y = jnp.concatenate([jnp.zeros((MB, NX, 1), jnp.float32), flux_y[:, :, :-1]], axis=2)
        return -(flux_x - prev_x) - (flux_y - prev_y)

    result = lax.map(one_block, jnp.arange(N_MODE, dtype=jnp.int32))
    return result.reshape(MODES, NX, NY)
```

```python
import functools

import jax
import jax.numpy as jnp
from jax import lax
from jax.experimental import pallas as pl
from jax.experimental.pallas import tpu as pltpu
from jax.sharding import PartitionSpec as P

LANES = 512


def kernel(n_mode, n_space, field_hbm, kx_hbm, ky_hbm, coup_hbm, pat_hbm, out_ref,
           raw, tall, u_ext, v_ext, kx_ref, ky_ref, coup, pat, packed, packed_in, pair_ref,
           kx_in, fx_prev, fy_row, held, last_row, sh,
           local_sem, main_send, main_recv, halo_send, halo_recv):
    mb, rows, ny = field_hbm.shape
    group = 128 // mb
    terms = kx_hbm.shape[0]
    sides = v_ext.shape[0]
    mode = lax.axis_index("mode")
    space = lax.axis_index("space")
    above = {"space": lax.rem(space + 1, n_space)}
    below = {"space": lax.rem(space + n_space - 1, n_space)}
    upper = {"mode": lax.rem(mode + 1, n_mode)}
    lower = {"mode": lax.rem(mode + n_mode - 1, n_mode)}

    barrier = pltpu.get_barrier_semaphore()
    has_below = space > 0
    has_above = space < n_space - 1

    def greet(target):
        pl.semaphore_signal(barrier, inc=1, device_id=target, device_id_type=pl.DeviceIdType.MESH)

    for target in (upper, lower)[:sides]:
        greet(target)
    pl.when(has_below)(lambda: greet(below))
    pl.when(has_above)(lambda: greet(above))
    locals_ = [
        pltpu.make_async_copy(src, dst, local_sem.at[i])
        for i, (src, dst) in enumerate([
            (field_hbm.at[:, pl.ds(0, 8), :], raw.at[:, pl.ds(0, 8), :]),
            (field_hbm.at[:, pl.ds(8, rows - 8), :], raw.at[:, pl.ds(8, rows - 8), :]),
            (coup_hbm, coup), (pat_hbm, pat), (kx_hbm, kx_ref), (ky_hbm, ky_ref)])]
    for copy in locals_:
        copy.start()

    def masked(slot, k):
        return jnp.where(pat[slot, k] > 0, coup[slot, k].astype(jnp.float32), 0.0)

    def placed(block, shape, offset, flip=False):
        spot = lax.broadcasted_iota(jnp.int32, shape, 0) + offset
        place = jnp.where(lax.broadcasted_iota(jnp.int32, shape, 1) == spot, 1.0, 0.0).astype(jnp.bfloat16)
        return lax.dot_general(block.astype(jnp.bfloat16), place, (((0 if flip else 1,), (0,)), ((), ())),
                               preferred_element_type=jnp.float32)

    def by_rows(first, count):
        for c in range(0, ny, 128):
            tall[:mb * count] = raw[:, first:first + count, c:c + 128].astype(jnp.float32).reshape(mb * count, 128)
            for r in range(count):
                u_ext[first + r + 1, :, c:c + 128] = tall[pl.ds(r, mb, stride=count), :].astype(jnp.bfloat16)

    locals_[0].wait()
    by_rows(0, 8)
    pl.semaphore_wait(barrier, sides + jnp.where(has_below, 1, 0) + jnp.where(has_above, 1, 0))

    def remote(src, dst, send, recv, target):
        return pltpu.make_async_remote_copy(
            src_ref=src, dst_ref=dst, send_sem=send, recv_sem=recv,
            device_id=target, device_id_type=pl.DeviceIdType.MESH)

    towards = (lower, upper)

    def row_copy(side, r):
        return remote(u_ext.at[r + 1], v_ext.at[side, r + 1], main_send.at[side, r], main_recv.at[side, r], towards[side])

    def halo_up(side):
        return remote(v_ext.at[side, rows], v_ext.at[side, 0], halo_send.at[4 + side], halo_recv.at[4 + side], above)

    def halo_down(side):
        return remote(v_ext.at[side, 1], v_ext.at[side, rows + 1], halo_send.at[6 + side], halo_recv.at[6 + side], below)

    coup_copy = remote(packed, packed_in, halo_send.at[0], halo_recv.at[0], upper)
    last_copy = remote(u_ext.at[rows], u_ext.at[0], halo_send.at[1], halo_recv.at[1], above)
    first_copy = remote(u_ext.at[1], u_ext.at[rows + 1], halo_send.at[2], halo_recv.at[2], below)
    kx_copy = remote(kx_hbm.at[:, pl.ds(rows - 8, 8), :], kx_in, halo_send.at[3], halo_recv.at[3], above)

    for side in range(sides):
        row_copy(side, 0).start()
    pl.when(has_below)(first_copy.start)
    pl.when(has_above)(kx_copy.start)
    locals_[1].wait()
    by_rows(8, rows - 8)
    for side in range(sides):
        row_copy(side, rows - 1).start()
        row_copy(side, 1).start()
        row_copy(side, 2).start()
    pl.when(has_above)(last_copy.start)

    locals_[2].wait()
    locals_[3].wait()
    for q in range(terms // group):
        beside = None
        for p in range(group):
            part = placed(masked(1, q * group + p), (mb, 128), p * mb, flip=True)
            beside = part if beside is None else beside + part
        packed[q * mb:(q + 1) * mb] = beside.astype(jnp.bfloat16)

    coup_copy.start()
    for side in range(sides):
        @pl.loop(3, rows - 1)
        def _(r):
            row_copy(side, r).start()

    for side in range(sides):
        row_copy(side, 0).wait_recv()
        pl.when(has_below)(halo_down(side).start)
        row_copy(side, rows - 1).wait_recv()
        pl.when(has_above)(halo_up(side).start)
    coup_copy.wait_recv()
    for copy in locals_[4:]:
        copy.wait()

    for k in range(terms):
        q, p = divmod(k, group)
        half = masked(0, k) * 0.5
        shape = (mb, 4 * mb)
        coef = (placed(half, shape, 0) + placed(half, shape, mb, flip=True) + placed(masked(1, k), shape, 2 * mb)
                + placed(packed_in[q * mb:(q + 1) * mb, p * mb:(p + 1) * mb], shape, 3 * mb)).astype(jnp.bfloat16)
        pair_ref[k * mb:(k + 1) * mb, :4 * mb] = coef
        pair_ref[k * mb:(k + 1) * mb, 4 * mb:] = -coef

    @pl.when(has_below)
    def _():
        last_copy.wait_recv()
        kx_copy.wait_recv()
        for side in range(sides):
            halo_up(side).wait_recv()

    @pl.when(has_above)
    def _():
        first_copy.wait_recv()
        for side in range(sides):
            halo_down(side).wait_recv()

    def blank(e):
        u_ext[e] = jnp.zeros((mb, ny), jnp.bfloat16)
        for side in range(sides):
            v_ext[side, e] = jnp.zeros((mb, ny), jnp.bfloat16)

    @pl.when(jnp.logical_not(has_below))
    def _():
        blank(0)
        kx_in[...] = jnp.zeros_like(kx_in)

    @pl.when(jnp.logical_not(has_above))
    def _():
        blank(rows + 1)

    pair = pair_ref[...]

    def stack(e, cols):
        u = u_ext[e, :, cols]
        vs = [v_ext[side, e, :, cols] for side in range(sides)]
        return [u, u, vs[0], vs[-1]]

    def weighted(diff, weight_of):
        total = None
        for k in range(terms):
            part = weight_of(k) * diff[k * mb:(k + 1) * mb]
            total = part if total is None else total + part
        return total

    def flux_x(e, cols, weight_of):
        diff = jnp.dot(pair, jnp.concatenate(stack(e + 1, cols) + stack(e, cols), axis=0),
                       preferred_element_type=jnp.float32)
        return weighted(diff, weight_of)

    blocks = [pl.ds(c, LANES) for c in range(0, ny, LANES)]
    for cols in blocks:
        fx_prev[:, cols] = flux_x(0, cols, lambda k: kx_in[k, 7:8, cols])

    def shifted(x):
        lane = lax.broadcasted_iota(jnp.int32, x.shape, 1)
        moved = pltpu.roll(x.astype(jnp.float32), ny - 1, axis=1)
        return jnp.where(lane == ny - 1, 0.0, moved).astype(jnp.bfloat16)

    def kx_row(r, cols):
        return lambda k: kx_ref[k, pl.ds(r, 1), cols]

    def flux_y_part(r):
        e = r + 1
        sh[0] = shifted(u_ext[e])
        for side in range(sides):
            sh[1 + side] = shifted(v_ext[side, e])
        for cols in blocks:
            ahead = [sh[0, :, cols]] * 2 + [sh[1, :, cols], sh[sides, :, cols]]
            diff = jnp.dot(pair, jnp.concatenate(ahead + stack(e, cols), axis=0),
                           preferred_element_type=jnp.float32)
            fy_row[:, cols] = weighted(diff, lambda k: ky_ref[k, pl.ds(r, 1), cols])
        fy = fy_row[...]
        lane = lax.broadcasted_iota(jnp.int32, fy.shape, 1)
        return jnp.where(lane == 0, 0.0, pltpu.roll(fy, 1, axis=1)) - fy

    def put(r, cols, value):
        for at in range(0, LANES, 128):
            tile = (cols.start + at) // 128
            start = (r // 8) * 8 * (ny // 128) + tile * 8 + r % 8
            out_ref[pl.ds(start, mb, stride=rows * (ny // 128)), :] = value[:, at:at + 128]

    def flux_x_step(r):
        for cols in blocks:
            fx = flux_x(r + 1, cols, kx_row(r, cols))
            put(r, cols, fx_prev[:, cols] - fx + held[:, cols])
            fx_prev[:, cols] = fx

    final = rows - 1
    last_row[...] = flux_y_part(final)
    for cols in blocks:
        last_row[:, cols] = last_row[:, cols] - flux_x(rows, cols, kx_row(final, cols))

    @pl.loop(0, rows - 3)
    def _(r):
        held[...] = flux_y_part(r)
        for side in range(sides):
            row_copy(side, r + 1).wait_recv()
        flux_x_step(r)

    held[...] = flux_y_part(rows - 3)
    for side in range(sides):
        row_copy(side, rows - 2).wait_recv()
    flux_x_step(rows - 3)
    held[...] = flux_y_part(rows - 2)
    flux_x_step(rows - 2)
    for cols in blocks:
        put(final, cols, last_row[:, cols] + fx_prev[:, cols])

    for side in range(sides):
        @pl.loop(0, rows)
        def _(r):
            row_copy(side, r).wait_send()
    coup_copy.wait_send()

    @pl.when(has_above)
    def _():
        for copy in (last_copy, kx_copy) + tuple(halo_up(side) for side in range(sides)):
            copy.wait_send()

    @pl.when(has_below)
    def _():
        for copy in (first_copy,) + tuple(halo_down(side) for side in range(sides)):
            copy.wait_send()


def shards(n_mode, n_space, field, kappa_x, kappa_y, coupling, pattern):
    mb, rows, ny = field.shape
    terms = kappa_x.shape[0]
    sides = 1 if n_mode == 2 else 2
    vmem = pl.BlockSpec(memory_space=pltpu.VMEM)
    hbm = pl.BlockSpec(memory_space=pltpu.HBM)
    out = pl.pallas_call(
        functools.partial(kernel, n_mode, n_space),
        out_shape=jax.ShapeDtypeStruct((mb * rows * ny // 128, 128), jnp.float32),
        in_specs=[hbm] * 5,
        out_specs=vmem,
        scratch_shapes=[
            pltpu.VMEM(field.shape, jnp.bfloat16),
            pltpu.VMEM((mb * rows, 128), jnp.float32),
            pltpu.VMEM((rows + 2, mb, ny), jnp.bfloat16),
            pltpu.VMEM((sides, rows + 2, mb, ny), jnp.bfloat16),
            pltpu.VMEM(kappa_x.shape, jnp.float32),
            pltpu.VMEM(kappa_y.shape, jnp.float32),
            pltpu.VMEM(coupling.shape, jnp.bfloat16),
            pltpu.VMEM(pattern.shape, jnp.int32),
            pltpu.VMEM((terms * mb * mb // 128, 128), jnp.bfloat16),
            pltpu.VMEM((terms * mb * mb // 128, 128), jnp.bfloat16),
            pltpu.VMEM((terms * mb, 8 * mb), jnp.bfloat16),
            pltpu.VMEM((terms, 8, ny), jnp.float32),
            pltpu.VMEM((mb, ny), jnp.float32),
            pltpu.VMEM((mb, ny), jnp.float32),
            pltpu.VMEM((mb, ny), jnp.float32),
            pltpu.VMEM((mb, ny), jnp.float32),
            pltpu.VMEM((1 + sides, mb, ny), jnp.bfloat16),
            pltpu.SemaphoreType.DMA((6,)),
            pltpu.SemaphoreType.DMA((sides, rows)),
            pltpu.SemaphoreType.DMA((sides, rows)),
            pltpu.SemaphoreType.DMA((9,)),
            pltpu.SemaphoreType.DMA((9,)),
        ],
        compiler_params=pltpu.CompilerParams(collective_id=0, has_side_effects=True, vmem_limit_bytes=24 * 2**20),
    )(*[pltpu.with_memory_space_constraint(x, pltpu.HBM)
        for x in (field, kappa_x, kappa_y, coupling, pattern)])
    tiles = out.reshape(mb, rows // 8, ny // 128, 8, 128)
    return jnp.swapaxes(tiles, 2, 3).reshape(mb, rows, ny)


def solution(mesh):
    placed = (
        P("mode", "space", None),
        P(None, "space", None),
        P(None, "space", None),
        P("mode", None, None, None),
        P("mode", None, None, None),
    )
    return jax.shard_map(
        functools.partial(shards, mesh.shape["mode"], mesh.shape["space"]),
        mesh=mesh, in_specs=placed, out_specs=P("mode", "space", None), check_vma=False)
```

```python
import functools

import jax
import jax.numpy as jnp
from jax import lax
from jax.experimental import pallas as pl
from jax.experimental.pallas import tpu as pltpu
from jax.sharding import PartitionSpec as P

LANES = 512
EARLY = 128
LATE = (384,)


def kernel(n_mode, n_space, field_hbm, kx_hbm, ky_hbm, coup_hbm, pat_hbm, out_ref,
           raw, raw_in, tall, u_ext, v_ext, kappa, coup, pat, packed, packed_in, pair_ref,
           kx_in, fx_prev, fy_row, held, first_row, last_row, ahead, sh,
           local_sem, field_send, early_recv, row_recv, piece_recv, other_send, other_recv):
    mb, rows, ny = field_hbm.shape
    group = 128 // mb
    terms = kx_hbm.shape[0]
    sides = v_ext.shape[0]
    early = raw_in.shape[-1]
    mode = lax.axis_index("mode")
    space = lax.axis_index("space")
    above = {"space": lax.rem(space + 1, n_space)}
    below = {"space": lax.rem(space + n_space - 1, n_space)}
    upper = {"mode": lax.rem(mode + 1, n_mode)}
    lower = {"mode": lax.rem(mode + n_mode - 1, n_mode)}
    has_below = space > 0
    has_above = space < n_space - 1
    kx_ref, ky_ref = kappa.at[0], kappa.at[1]

    barrier = pltpu.get_barrier_semaphore()

    def greet(target):
        pl.semaphore_signal(barrier, inc=1, device_id=target, device_id_type=pl.DeviceIdType.MESH)

    for target in (upper, lower)[:sides]:
        greet(target)
    pl.when(has_above)(lambda: greet(above))

    field_load = pltpu.make_async_copy(field_hbm, raw, local_sem.at[0])
    coup_load = pltpu.make_async_copy(coup_hbm, coup, local_sem.at[1])
    pat_load = pltpu.make_async_copy(pat_hbm, pat, local_sem.at[2])
    kx_load = pltpu.make_async_copy(kx_hbm, kx_ref, local_sem.at[3])
    ky_load = pltpu.make_async_copy(ky_hbm, ky_ref, local_sem.at[3])
    for copy in (field_load, coup_load, pat_load, kx_load, ky_load):
        copy.start()

    def masked(slot, k):
        return jnp.where(pat[slot, k] > 0, coup[slot, k].astype(jnp.float32), 0.0)

    def placed(block, shape, offset, flip=False):
        spot = lax.broadcasted_iota(jnp.int32, shape, 0) + offset
        place = jnp.where(lax.broadcasted_iota(jnp.int32, shape, 1) == spot, 1.0, 0.0).astype(jnp.bfloat16)
        return lax.dot_general(block.astype(jnp.bfloat16), place, (((0 if flip else 1,), (0,)), ((), ())),
                               preferred_element_type=jnp.float32)

    def by_rows(source, target, first, count, width):
        for c in range(0, width, 128):
            tall[:mb * count] = source[:, first:first + count, c:c + 128].astype(jnp.float32).reshape(mb * count, 128)
            for r in range(count):
                target[first + r + 1, :, c:c + 128] = tall[pl.ds(r, mb, stride=count), :].astype(jnp.bfloat16)

    pl.semaphore_wait(barrier, sides + jnp.where(has_below, 1, 0))

    def remote(src, dst, send, recv, target):
        return pltpu.make_async_remote_copy(
            src_ref=src, dst_ref=dst, send_sem=send, recv_sem=recv,
            device_id=target, device_id_type=pl.DeviceIdType.MESH)

    towards = (lower, upper)
    cuts = [early] + [ny - w for w in LATE if ny - w > early] + [ny]
    pieces = list(zip(cuts[:-1], cuts[1:]))
    pairs = (rows - 6) // 2
    rest = pl.ds(early, ny - early)

    def rows_copy(side, first, count, at, cols=rest, recv=row_recv):
        part = pl.ds(first + 1, count)
        return remote(u_ext.at[part, :, cols], v_ext.at[side, part, :, cols],
                      field_send.at[side], recv.at[side, at], towards[side])

    def pair_copy(side, h):
        return rows_copy(side, 2 * h + 2, 2, h + 2)

    def single_copy(side, r):
        return rows_copy(side, r, 1, r - (rows - 4) + pairs + 2)

    def piece_copy(side, p):
        first, last = pieces[p]
        return rows_copy(side, rows - 2, 1, p, pl.ds(first, last - first), piece_recv)

    def early_copy(side):
        return remote(field_hbm.at[:, :, pl.ds(0, early)], raw_in.at[side], field_send.at[side], early_recv.at[side], towards[side])

    def halo_up(side):
        return remote(v_ext.at[side, rows], v_ext.at[side, 0], other_send.at[1], other_recv.at[1], above)

    def halo_down(side):
        return remote(v_ext.at[side, 1], v_ext.at[side, rows + 1], other_send.at[2], other_recv.at[2], below)

    coup_copy = remote(packed, packed_in, other_send.at[0], other_recv.at[0], upper)
    last_copy = remote(u_ext.at[rows], u_ext.at[0], other_send.at[1], other_recv.at[1], above)
    first_copy = remote(u_ext.at[1], u_ext.at[rows + 1], other_send.at[2], other_recv.at[3], below)
    kx_copy = remote(kx_hbm.at[:, pl.ds(rows - 8, 8), :], kx_in, other_send.at[3], other_recv.at[4], above)

    def strips(count, sem):
        part = u_ext.at[pl.ds(0, count)]
        return pltpu.make_async_copy(part, part, sem)

    for side in range(sides):
        early_copy(side).start()

    coup_load.wait()
    pat_load.wait()
    for q in range(terms // group):
        beside = None
        for p in range(group):
            part = placed(masked(1, q * group + p), (mb, 128), p * mb, flip=True)
            beside = part if beside is None else beside + part
        packed[q * mb:(q + 1) * mb] = beside.astype(jnp.bfloat16)
    coup_copy.start()

    field_load.wait()
    by_rows(raw, u_ext, 0, rows, ny)
    for side in range(sides):
        rows_copy(side, 0, 2, 0).start()
        rows_copy(side, rows - 1, 1, 1).start()
    pl.when(has_below)(first_copy.start)
    for side in range(sides):
        @pl.loop(0, pairs)
        def _(h):
            pair_copy(side, h).start()
    for r in (rows - 4, rows - 3):
        for side in range(sides):
            single_copy(side, r).start()
    for p in range(len(pieces)):
        for side in range(sides):
            piece_copy(side, p).start()

    for k in range(terms):
        half = masked(0, k) * 0.5
        shape = (mb, 4 * mb)
        coef = placed(half, shape, 0) + placed(half, shape, mb, flip=True) + placed(masked(1, k), shape, 2 * mb)
        pair_ref[k * mb:(k + 1) * mb, :4 * mb] = coef.astype(jnp.bfloat16)

    @pl.when(has_above)
    def _():
        first_copy.wait_recv()
        last_copy.start()
        kx_copy.start()

    for side in range(sides):
        early_copy(side).wait_recv()
        by_rows(raw_in.at[side], v_ext.at[side], 0, rows, early)
    coup_copy.wait_recv()
    pltpu.make_async_copy(kappa, kappa, local_sem.at[3]).wait()
    for k in range(terms):
        q, p = divmod(k, group)
        shape = (mb, 4 * mb)
        coef = (pair_ref[k * mb:(k + 1) * mb, :4 * mb].astype(jnp.float32)
                + placed(packed_in[q * mb:(q + 1) * mb, p * mb:(p + 1) * mb], shape, 3 * mb)).astype(jnp.bfloat16)
        pair_ref[k * mb:(k + 1) * mb, :4 * mb] = coef
        pair_ref[k * mb:(k + 1) * mb, 4 * mb:] = -coef
    for side in range(sides):
        rows_copy(side, 0, 2, 0).wait_recv()
        pl.when(has_below)(halo_down(side).start)
        rows_copy(side, rows - 1, 1, 1).wait_recv()
        pl.when(has_above)(halo_up(side).start)

    pair = pair_ref[...]

    def stack(e, cols):
        u = u_ext[e, :, cols]
        vs = [v_ext[side, e, :, cols] for side in range(sides)]
        return [u, u, vs[0], vs[-1]]

    def weighted(diff, weight_of):
        total = None
        for k in range(terms):
            part = weight_of(k) * diff[k * mb:(k + 1) * mb]
            total = part if total is None else total + part
        return total

    def flux_x(e, cols, weight_of):
        diff = jnp.dot(pair, jnp.concatenate(stack(e + 1, cols) + stack(e, cols), axis=0),
                       preferred_element_type=jnp.float32)
        return weighted(diff, weight_of)

    blocks = [pl.ds(c, LANES) for c in range(0, ny, LANES)]

    def shifted(x):
        lane = lax.broadcasted_iota(jnp.int32, x.shape, 1)
        moved = pltpu.roll(x.astype(jnp.float32), ny - 1, axis=1)
        return jnp.where(lane == ny - 1, 0.0, moved).astype(jnp.bfloat16)

    def kx_row(r, cols):
        return lambda k: kx_ref[k, pl.ds(r, 1), cols]

    def flux_y_part(r):
        e = r + 1
        sh[0] = shifted(u_ext[e])
        for side in range(sides):
            sh[1 + side] = shifted(v_ext[side, e])
        for cols in blocks:
            next_cols = [sh[0, :, cols]] * 2 + [sh[1, :, cols], sh[sides, :, cols]]
            diff = jnp.dot(pair, jnp.concatenate(next_cols + stack(e, cols), axis=0),
                           preferred_element_type=jnp.float32)
            fy_row[:, cols] = weighted(diff, lambda k: ky_ref[k, pl.ds(r, 1), cols])
        fy = fy_row[...]
        lane = lax.broadcasted_iota(jnp.int32, fy.shape, 1)
        return jnp.where(lane == 0, 0.0, pltpu.roll(fy, 1, axis=1)) - fy

    def put(r, cols, value):
        for at in range(0, cols.size, 128):
            tile = (cols.start + at) // 128
            start = (r // 8) * 8 * (ny // 128) + tile * 8 + r % 8
            out_ref[pl.ds(start, mb, stride=rows * (ny // 128)), :] = value[:, at:at + 128]

    def flux_x_step(r):
        for cols in blocks:
            fx = flux_x(r + 1, cols, kx_row(r, cols))
            put(r, cols, fx_prev[:, cols] - fx + held[:, cols])
            fx_prev[:, cols] = fx

    final = rows - 1

    def edges():
        @pl.when(has_below)
        def _():
            strips(1 + sides, other_recv.at[1]).wait()
            kx_copy.wait_recv()

        @pl.when(has_above)
        def _():
            strips(sides, other_recv.at[2]).wait()

        def blank(e):
            u_ext[e] = jnp.zeros((mb, ny), jnp.bfloat16)
            for side in range(sides):
                v_ext[side, e] = jnp.zeros((mb, ny), jnp.bfloat16)

        @pl.when(jnp.logical_not(has_below))
        def _():
            blank(0)
            kx_in[...] = jnp.zeros_like(kx_in)

        @pl.when(jnp.logical_not(has_above))
        def _():
            blank(rows + 1)

        last_row[...] = flux_y_part(final)
        for cols in blocks:
            put(0, cols, first_row[:, cols] + flux_x(0, cols, lambda k: kx_in[k, 7:8, cols]))
            last_row[:, cols] = last_row[:, cols] - flux_x(rows, cols, kx_row(final, cols))

    first_row[...] = flux_y_part(0)
    for cols in blocks:
        fx = flux_x(1, cols, kx_row(0, cols))
        first_row[:, cols] = first_row[:, cols] - fx
        fx_prev[:, cols] = fx
    held[...] = flux_y_part(1)

    @pl.loop(0, pairs)
    def _(h):
        pl.when(h == pairs // 2)(edges)
        for side in range(sides):
            pair_copy(side, h).wait_recv()
        r = 2 * h + 1
        flux_x_step(r)
        held[...] = flux_y_part(r + 1)
        flux_x_step(r + 1)
        held[...] = flux_y_part(r + 2)

    @pl.loop(rows - 4, rows - 2)
    def _(r):
        for side in range(sides):
            single_copy(side, r).wait_recv()
        flux_x_step(r - 1)
        held[...] = flux_y_part(r)

    late = rows - 2

    def ahead_of(x, width):
        turned = pltpu.roll(x.astype(jnp.float32), x.shape[1] - 1, axis=1)
        if x.shape[1] == width:
            lane = lax.broadcasted_iota(jnp.int32, x.shape, 1)
            turned = jnp.where(lane == width - 1, 0.0, turned)
        return turned[:, :width].astype(jnp.bfloat16)

    for p, (first, last) in enumerate(pieces):
        first = 0 if p == 0 else first
        width = last - first
        cols = pl.ds(first, width)
        y_first = max(first - 128, 0)
        y_last = last if last == ny else last - 128
        y_width = y_last - y_first
        y_cols = pl.ds(y_first, y_width)
        more = pl.ds(y_first, min(y_width + 128, ny - y_first))
        for side in range(sides):
            piece_copy(side, p).wait_recv()
        u_next = ahead_of(u_ext[late + 1, :, more], y_width)
        v_next = [ahead_of(v_ext[side, late + 1, :, more], y_width) for side in range(sides)]
        columns = [stack(late + 1, cols) + stack(late, cols), stack(late + 2, cols) + stack(late + 1, cols),
                   [u_next, u_next, v_next[0], v_next[-1]] + stack(late + 1, y_cols)]
        diff = jnp.dot(pair, jnp.concatenate([jnp.concatenate(c, axis=0) for c in columns], axis=1),
                       preferred_element_type=jnp.float32)
        mid = weighted(diff[:, :width], kx_row(late - 1, cols))
        top = weighted(diff[:, width:2 * width], kx_row(late, cols))
        fy = weighted(diff[:, 2 * width:], lambda k: ky_ref[k, pl.ds(late, 1), y_cols])
        put(late - 1, cols, fx_prev[:, cols] - mid + held[:, cols])
        put(final, cols, last_row[:, cols] + top)
        if p == 0:
            lane = lax.broadcasted_iota(jnp.int32, fy.shape, 1)
            part = jnp.where(lane == 0, 0.0, pltpu.roll(fy, 1, axis=1)) - fy
            keep = mid - top
        else:
            both = jnp.concatenate([fy_row[:, y_first - 128:y_first], fy], axis=1)
            part = pltpu.roll(both, 1, axis=1)[:, 128:] - fy
            keep = jnp.concatenate([ahead[:, y_first:first], mid - top], axis=1)
        put(late, y_cols, keep[:, :y_width] + part)
        if last < ny:
            ahead[:, y_last:last] = keep[:, y_width:]
            fy_row[:, y_last - 128:y_last] = fy[:, y_width - 128:]

    for side in range(sides):
        pltpu.make_async_copy(raw, raw, field_send.at[side]).wait()
    coup_copy.wait_send()

    @pl.when(has_above)
    def _():
        strips(1 + sides, other_send.at[1]).wait()
        kx_copy.wait_send()

    @pl.when(has_below)
    def _():
        strips(1 + sides, other_send.at[2]).wait()


def shards(n_mode, n_space, field, kappa_x, kappa_y, coupling, pattern):
    mb, rows, ny = field.shape
    terms = kappa_x.shape[0]
    sides = 1 if n_mode == 2 else 2
    vmem = pl.BlockSpec(memory_space=pltpu.VMEM)
    hbm = pl.BlockSpec(memory_space=pltpu.HBM)
    out = pl.pallas_call(
        functools.partial(kernel, n_mode, n_space),
        out_shape=jax.ShapeDtypeStruct((mb * rows * ny // 128, 128), jnp.float32),
        in_specs=[hbm] * 5,
        out_specs=vmem,
        scratch_shapes=[
            pltpu.VMEM(field.shape, jnp.bfloat16),
            pltpu.VMEM((sides, mb, rows, min(EARLY, ny // 2)), jnp.bfloat16),
            pltpu.VMEM((mb * rows, 128), jnp.float32),
            pltpu.VMEM((rows + 2, mb, ny), jnp.bfloat16),
            pltpu.VMEM((sides, rows + 2, mb, ny), jnp.bfloat16),
            pltpu.VMEM((2,) + kappa_x.shape, jnp.float32),
            pltpu.VMEM(coupling.shape, jnp.bfloat16),
            pltpu.VMEM(pattern.shape, jnp.int32),
            pltpu.VMEM((terms * mb * mb // 128, 128), jnp.bfloat16),
            pltpu.VMEM((terms * mb * mb // 128, 128), jnp.bfloat16),
            pltpu.VMEM((terms * mb, 8 * mb), jnp.bfloat16),
            pltpu.VMEM((terms, 8, ny), jnp.float32),
            pltpu.VMEM((mb, ny), jnp.float32),
            pltpu.VMEM((mb, ny), jnp.float32),
            pltpu.VMEM((mb, ny), jnp.float32),
            pltpu.VMEM((mb, ny), jnp.float32),
            pltpu.VMEM((mb, ny), jnp.float32),
            pltpu.VMEM((mb, ny), jnp.float32),
            pltpu.VMEM((1 + sides, mb, ny), jnp.bfloat16),
            pltpu.SemaphoreType.DMA((4,)),
            pltpu.SemaphoreType.DMA((sides,)),
            pltpu.SemaphoreType.DMA((sides,)),
            pltpu.SemaphoreType.DMA((sides, rows // 2 + 1)),
            pltpu.SemaphoreType.DMA((sides, 1 + len(LATE))),
            pltpu.SemaphoreType.DMA((4,)),
            pltpu.SemaphoreType.DMA((5,)),
        ],
        compiler_params=pltpu.CompilerParams(collective_id=0, has_side_effects=True, vmem_limit_bytes=24 * 2**20),
    )(*[pltpu.with_memory_space_constraint(x, pltpu.HBM)
        for x in (field, kappa_x, kappa_y, coupling, pattern)])
    tiles = out.reshape(mb, rows // 8, ny // 128, 8, 128)
    return jnp.swapaxes(tiles, 2, 3).reshape(mb, rows, ny)


def solution(mesh):
    placed = (
        P("mode", "space", None),
        P(None, "space", None),
        P(None, "space", None),
        P("mode", None, None, None),
        P("mode", None, None, None),
    )
    return jax.shard_map(
        functools.partial(shards, mesh.shape["mode"], mesh.shape["space"]),
        mesh=mesh, in_specs=placed, out_specs=P("mode", "space", None), check_vma=False)
```

```python
import functools

import jax
import jax.numpy as jnp
from jax import lax
from jax.experimental import pallas as pl
from jax.experimental.pallas import tpu as pltpu
from jax.sharding import PartitionSpec as P

LANES = 256
PART = 16
EARLY = 128
LATE = (384,)


def kernel(n_mode, n_space, field_hbm, kx_hbm, ky_hbm, coup_hbm, pat_hbm, out_ref,
           raw, raw_in, tall, u_ext, v_ext, kappa, ky_left, coup, pat, packed, packed_in, relay, own_ref, mixed_ref, coef_ref,
           kx_in, pend, low, q_row, z_row, first_row, last_row, high,
           local_sem, field_send, early_recv, row_recv, piece_recv, other_send, other_recv, relay_sem, hello):
    mb, rows, ny = field_hbm.shape
    group = 128 // mb
    terms = kx_hbm.shape[0]
    sides = v_ext.shape[0]
    early = raw_in.shape[-1]
    mode = lax.axis_index("mode")
    space = lax.axis_index("space")
    above = {"space": lax.rem(space + 1, n_space)}
    below = {"space": lax.rem(space + n_space - 1, n_space)}
    upper = {"mode": lax.rem(mode + 1, n_mode)}
    lower = {"mode": lax.rem(mode + n_mode - 1, n_mode)}
    has_below = space > 0
    has_above = space < n_space - 1
    kx_ref, ky_ref = kappa.at[0], kappa.at[1]

    barrier = pltpu.get_barrier_semaphore()

    def greet(target):
        pl.semaphore_signal(barrier, inc=1, device_id=target, device_id_type=pl.DeviceIdType.MESH)

    for target in (upper, lower)[:sides]:
        greet(target)
    pl.when(has_above)(lambda: greet(above))

    field_load = pltpu.make_async_copy(field_hbm, raw, local_sem.at[0])
    coup_load = pltpu.make_async_copy(coup_hbm, coup, local_sem.at[1])
    pat_load = pltpu.make_async_copy(pat_hbm, pat, local_sem.at[2])
    kx_load = pltpu.make_async_copy(kx_hbm, kx_ref, local_sem.at[3])
    ky_load = pltpu.make_async_copy(ky_hbm, ky_ref, local_sem.at[3])
    for copy in (field_load, coup_load, pat_load, kx_load, ky_load):
        copy.start()

    def masked(slot, k):
        return jnp.where(pat[slot, k] > 0, coup[slot, k].astype(jnp.float32), 0.0)

    def placed(block, shape, offset, flip=False):
        spot = lax.broadcasted_iota(jnp.int32, shape, 0) + offset
        place = jnp.where(lax.broadcasted_iota(jnp.int32, shape, 1) == spot, 1.0, 0.0).astype(jnp.bfloat16)
        return lax.dot_general(block.astype(jnp.bfloat16), place, (((0 if flip else 1,), (0,)), ((), ())),
                               preferred_element_type=jnp.float32)

    def by_rows(source, target, first, count, width):
        for c in range(0, width, 128):
            tall[:mb * count] = source[:, first:first + count, c:c + 128].astype(jnp.float32).reshape(mb * count, 128)
            for r in range(count):
                target[first + r + 1, :, c:c + 128] = tall[pl.ds(r, mb, stride=count), :].astype(jnp.bfloat16)

    pl.semaphore_wait(barrier, sides + jnp.where(has_below, 1, 0))

    @pl.when(has_below)
    def _():
        pl.semaphore_signal(hello, inc=1, device_id=below, device_id_type=pl.DeviceIdType.MESH)

    def remote(src, dst, send, recv, target):
        return pltpu.make_async_remote_copy(
            src_ref=src, dst_ref=dst, send_sem=send, recv_sem=recv,
            device_id=target, device_id_type=pl.DeviceIdType.MESH)

    towards = (lower, upper)
    cuts = [early] + [ny - w for w in LATE if ny - w > early] + [ny]
    pieces = list(zip(cuts[:-1], cuts[1:]))
    pairs = (rows - 6) // 2
    rest = pl.ds(early, ny - early)

    def rows_copy(side, first, count, at, cols=rest, recv=row_recv):
        part = pl.ds(first + 1, count)
        return remote(u_ext.at[part, :, cols], v_ext.at[side, part, :, cols],
                      field_send.at[side], recv.at[side, at], towards[side])

    def pair_copy(side, h):
        return rows_copy(side, 2 * h + 2, 2, h + 2)

    def single_copy(side, r):
        return rows_copy(side, r, 1, r - (rows - 4) + pairs + 2)

    def piece_copy(side, p):
        first, last = pieces[p]
        return rows_copy(side, rows - 2, 1, p, pl.ds(first, last - first), piece_recv)

    def early_copy(side):
        return remote(field_hbm.at[:, :, pl.ds(0, early)], raw_in.at[side], field_send.at[side], early_recv.at[side], towards[side])

    def halo_up(side):
        return remote(v_ext.at[side, rows], v_ext.at[side, 0], other_send.at[1], other_recv.at[1], above)

    def halo_down(side):
        return remote(v_ext.at[side, 1], v_ext.at[side, rows + 1], other_send.at[2], other_recv.at[2], below)

    shared = n_space % 2 == 0
    sends_coup = lax.rem(space, 2) == 0 if shared else space >= 0
    coup_pass = remote(packed_in, packed_in, other_send.at[4], other_recv.at[0], above)
    coup_copy = remote(packed, packed_in, other_send.at[0], other_recv.at[0], upper)
    last_copy = remote(u_ext.at[rows], u_ext.at[0], other_send.at[1], other_recv.at[1], above)
    first_copy = remote(u_ext.at[1], u_ext.at[rows + 1], other_send.at[2], other_recv.at[2], below)
    kx_copy = remote(kx_hbm.at[:, pl.ds(rows - 8, 8), :], kx_in, other_send.at[3], other_recv.at[3], above)

    def strips(count, sem):
        part = u_ext.at[pl.ds(0, count)]
        return pltpu.make_async_copy(part, part, sem)

    for side in range(sides):
        early_copy(side).start()

    coup_load.wait()
    pat_load.wait()

    @pl.when(sends_coup)
    def _():
        for q in range(terms // group):
            beside = None
            for p in range(group):
                part = placed(masked(1, q * group + p), (mb, 128), p * mb, flip=True)
                beside = part if beside is None else beside + part
            packed[q * mb:(q + 1) * mb] = beside.astype(jnp.bfloat16)
        coup_copy.start()

    field_load.wait()
    by_rows(raw, u_ext, 0, rows, ny)
    pl.when(has_above)(lambda: pl.semaphore_wait(hello, 1))

    detour = sides == 1 and n_space > 2
    gone = rows - 3
    source = (mode == 1) & (space == 1)
    middle = (mode == 1) & (space == 2)
    turn = (mode == 0) & (space == 2)
    yields = (mode == 1) & ((space == 1) | (space == 3))
    leave_copy = remote(u_ext.at[pl.ds(gone + 1, 1), :, rest], relay, field_send.at[0], relay_sem.at[0], above)
    cross_copy = remote(relay, relay, relay_sem.at[1], relay_sem.at[0], upper)
    come_copy = remote(relay, v_ext.at[0, pl.ds(gone + 1, 1), :, rest], relay_sem.at[1], row_recv.at[0, pairs + 3], below)

    if detour:
        pl.when(source)(leave_copy.start)
    for side in range(sides):
        rows_copy(side, 0, 2, 0).start()
    pl.when(has_below)(first_copy.start)
    if detour:
        @pl.when(middle)
        def _():
            leave_copy.wait_recv()
            cross_copy.start()
    for side in range(sides):
        rows_copy(side, rows - 1, 1, 1).start()
    if detour:
        @pl.when(turn)
        def _():
            cross_copy.wait_recv()
            come_copy.start()

    def send_rest():
        for side in range(sides):
            @pl.loop(0, pairs)
            def _(h):
                pair_copy(side, h).start()
        for r in (rows - 4, rows - 3):
            for side in range(sides):
                if detour and r == gone:
                    pl.when(jnp.logical_not(source))(single_copy(side, r).start)
                else:
                    single_copy(side, r).start()
        for p in range(len(pieces)):
            for side in range(sides):
                piece_copy(side, p).start()

        @pl.when(has_above)
        def _():
            last_copy.start()
            kx_copy.start()

    if detour:
        pl.when(jnp.logical_not(yields))(send_rest)
    else:
        send_rest()

    for k in range(terms):
        half = masked(0, k) * 0.5
        shape = (mb, 4 * mb)
        coef = placed(half, shape, 0) + placed(half, shape, mb, flip=True) + placed(masked(1, k), shape, 2 * mb)
        own_ref[k * mb:(k + 1) * mb] = coef

    for side in range(sides):
        early_copy(side).wait_recv()
    for side in range(sides):
        by_rows(raw_in.at[side], v_ext.at[side], 0, rows, early)
    coup_copy.wait_recv()
    if shared:
        pl.when(sends_coup)(coup_pass.start)
    pltpu.make_async_copy(kappa, kappa, local_sem.at[3]).wait()
    for k in range(terms):
        lane = lax.broadcasted_iota(jnp.int32, (rows, ny), 1)
        ky_left[k] = jnp.where(lane == 0, 0.0, pltpu.roll(ky_ref[k], 1, axis=1))
    for k in range(terms):
        q, p = divmod(k, group)
        shape = (mb, 4 * mb)
        coef = (own_ref[k * mb:(k + 1) * mb]
                + placed(packed_in[q * mb:(q + 1) * mb, p * mb:(p + 1) * mb], shape, 3 * mb))
        for m in range(0, mb, PART):
            own_at = m * terms + k * PART
            mixed_ref[own_at:own_at + PART] = coef[m:m + PART]
    coef_ref[...] = mixed_ref[...].astype(jnp.bfloat16)
    for side in range(sides):
        rows_copy(side, 0, 2, 0).wait_recv()
        pl.when(has_below)(halo_down(side).start)
    if detour:
        pl.when(yields)(send_rest)
    for side in range(sides):
        rows_copy(side, rows - 1, 1, 1).wait_recv()
        pl.when(has_above)(halo_up(side).start)

    coef = coef_ref[...]
    final = rows - 1
    late = rows - 2

    def w_of(e, cols):
        u = u_ext[e, :, cols]
        vs = [v_ext[side, e, :, cols] for side in range(sides)]
        return jnp.dot(coef, jnp.concatenate([u, u, vs[0], vs[-1]], axis=0), preferred_element_type=jnp.float32)

    def sums(w, *weights):
        parts = [[] for _ in weights]
        scales = [[weight(k) for k in range(terms)] for weight in weights]
        for m in range(0, mb, PART):
            totals = [None] * len(weights)
            for k in range(terms):
                part = w[m * terms + k * PART:m * terms + (k + 1) * PART]
                for i in range(len(weights)):
                    value = scales[i][k] * part
                    totals[i] = value if totals[i] is None else totals[i] + value
            for i in range(len(weights)):
                parts[i].append(totals[i])
        return [jnp.concatenate(p, axis=0) for p in parts]

    def row_of(ref, r, cols):
        return lambda k: ref[k, pl.ds(r, 1), cols]

    def from_left(q):
        lane = lax.broadcasted_iota(jnp.int32, q.shape, 1)
        return jnp.where(lane == 0, 0.0, pltpu.roll(q, 1, axis=1))

    def from_right(z):
        lane = lax.broadcasted_iota(jnp.int32, z.shape, 1)
        return jnp.where(lane == z.shape[1] - 1, 0.0, pltpu.roll(z, z.shape[1] - 1, axis=1))

    blocks = [pl.ds(c, LANES) for c in range(0, ny, LANES)]

    def put(r, cols, value):
        for at in range(0, cols.size, 128):
            tile = (cols.start + at) // 128
            start = (r // 8) * 8 * (ny // 128) + tile * 8 + r % 8
            out_ref[pl.ds(start, mb, stride=rows * (ny // 128)), :] = value[:, at:at + 128]

    def row_step(r, give):
        for cols in blocks:
            a, b, q, z = sums(w_of(r + 1, cols), row_of(kx_ref, r - 1, cols), row_of(kx_ref, r, cols),
                              row_of(ky_ref, r, cols), row_of(ky_left, r, cols))
            give(cols, a)
            pend[:, cols] = a + b + q + z - low[:, cols]
            low[:, cols] = b
            q_row[:, cols] = q
            z_row[:, cols] = z
        pend[...] = pend[...] - from_left(q_row[...]) - from_right(z_row[...])

    def full_step(r):
        row_step(r, lambda cols, a: put(r - 1, cols, pend[:, cols] - a))

    def edges():
        @pl.when(has_below)
        def _():
            strips(1 + sides, other_recv.at[1]).wait()
            kx_copy.wait_recv()

        @pl.when(has_above)
        def _():
            strips(1 + sides, other_recv.at[2]).wait()

        def blank(e):
            u_ext[e] = jnp.zeros((mb, ny), jnp.bfloat16)
            for side in range(sides):
                v_ext[side, e] = jnp.zeros((mb, ny), jnp.bfloat16)

        @pl.when(jnp.logical_not(has_below))
        def _():
            blank(0)
            kx_in[...] = jnp.zeros_like(kx_in)

        @pl.when(jnp.logical_not(has_above))
        def _():
            blank(rows + 1)

        for cols in blocks:
            outer = lambda k: kx_in[k, 7:8, cols]
            put(0, cols, first_row[:, cols] + sums(w_of(1, cols), outer)[0] - sums(w_of(0, cols), outer)[0])
            a, b, q, z = sums(w_of(rows, cols), row_of(kx_ref, late, cols), row_of(kx_ref, final, cols),
                              row_of(ky_ref, final, cols), row_of(ky_left, final, cols))
            last_row[:, cols] = a + b + q + z - sums(w_of(rows + 1, cols), row_of(kx_ref, final, cols))[0]
            high[:, cols] = a
            first_row[:, cols] = q
            z_row[:, cols] = z
        last_row[...] = last_row[...] - from_left(first_row[...]) - from_right(z_row[...])

    for cols in blocks:
        b, q, z = sums(w_of(1, cols), row_of(kx_ref, 0, cols), row_of(ky_ref, 0, cols), row_of(ky_left, 0, cols))
        low[:, cols] = b
        first_row[:, cols] = b + q + z
        q_row[:, cols] = q
        z_row[:, cols] = z
    first_row[...] = first_row[...] - from_left(q_row[...]) - from_right(z_row[...])

    def take_first(cols, a):
        first_row[:, cols] = first_row[:, cols] - a

    row_step(1, take_first)

    @pl.loop(0, pairs)
    def _(h):
        pl.when(h == pairs // 2)(edges)
        for side in range(sides):
            pair_copy(side, h).wait_recv()
        full_step(2 * h + 2)
        full_step(2 * h + 3)

    @pl.loop(rows - 4, rows - 2)
    def _(r):
        for side in range(sides):
            single_copy(side, r).wait_recv()
        full_step(r)

    high[...] = high[...] + low[...]

    for p, (first, last) in enumerate(pieces):
        first = 0 if p == 0 else first
        width = last - first
        cols = pl.ds(first, width)
        for side in range(sides):
            piece_copy(side, p).wait_recv()
        a, b, q, z = sums(w_of(late + 1, cols), row_of(kx_ref, late - 1, cols), row_of(kx_ref, late, cols),
                          row_of(ky_ref, late, cols), row_of(ky_left, late, cols))
        put(late - 1, cols, pend[:, cols] - a)
        put(final, cols, last_row[:, cols] - b)
        total = a + b + q + z - high[:, cols]
        y_first = max(first - 128, 0)
        y_last = last if last == ny else last - 128
        y_width = y_last - y_first
        if p > 0:
            before = pl.ds(y_first, 128)
            total = jnp.concatenate([low[:, before], total], axis=1)
            z = jnp.concatenate([z_row[:, before], z], axis=1)
            left = pltpu.roll(jnp.concatenate([q_row[:, y_first - 128:first], q], axis=1), 1, axis=1)[:, 128:]
        else:
            left = from_left(q)
        right = from_right(z) if last == ny else pltpu.roll(z, z.shape[1] - 1, axis=1)
        put(late, pl.ds(y_first, y_width), (total - left - right)[:, :y_width])
        if last < ny:
            after = pl.ds(y_last, 128)
            low[:, after] = total[:, y_width:]
            z_row[:, after] = z[:, y_width:]
            q_row[:, y_last - 128:last] = q[:, q.shape[1] - 256:]

    for side in range(sides):
        pltpu.make_async_copy(raw, raw, field_send.at[side]).wait()
    if detour:
        pl.when(middle | turn)(cross_copy.wait_send)

    @pl.when(sends_coup)
    def _():
        coup_copy.wait_send()
        if shared:
            coup_pass.wait_send()

    @pl.when(has_above)
    def _():
        strips(1 + sides, other_send.at[1]).wait()
        kx_copy.wait_send()

    @pl.when(has_below)
    def _():
        strips(1 + sides, other_send.at[2]).wait()


def shards(n_mode, n_space, field, kappa_x, kappa_y, coupling, pattern):
    mb, rows, ny = field.shape
    terms = kappa_x.shape[0]
    sides = 1 if n_mode == 2 else 2
    vmem = pl.BlockSpec(memory_space=pltpu.VMEM)
    hbm = pl.BlockSpec(memory_space=pltpu.HBM)
    out = pl.pallas_call(
        functools.partial(kernel, n_mode, n_space),
        out_shape=jax.ShapeDtypeStruct((mb * rows * ny // 128, 128), jnp.float32),
        in_specs=[hbm] * 5,
        out_specs=vmem,
        scratch_shapes=[
            pltpu.VMEM(field.shape, jnp.bfloat16),
            pltpu.VMEM((sides, mb, rows, min(EARLY, ny // 2)), jnp.bfloat16),
            pltpu.VMEM((mb * rows, 128), jnp.float32),
            pltpu.VMEM((rows + 2, mb, ny), jnp.bfloat16),
            pltpu.VMEM((sides, rows + 2, mb, ny), jnp.bfloat16),
            pltpu.VMEM((2,) + kappa_x.shape, jnp.float32),
            pltpu.VMEM(kappa_y.shape, jnp.float32),
            pltpu.VMEM(coupling.shape, jnp.bfloat16),
            pltpu.VMEM(pattern.shape, jnp.int32),
            pltpu.VMEM((terms * mb * mb // 128, 128), jnp.bfloat16),
            pltpu.VMEM((terms * mb * mb // 128, 128), jnp.bfloat16),
            pltpu.VMEM((1, mb, ny - min(EARLY, ny // 2)), jnp.bfloat16),
            pltpu.VMEM((terms * mb, 4 * mb), jnp.float32),
            pltpu.VMEM((terms * mb, 4 * mb), jnp.float32),
            pltpu.VMEM((terms * mb, 4 * mb), jnp.bfloat16),
            pltpu.VMEM((terms, 8, ny), jnp.float32),
            pltpu.VMEM((mb, ny), jnp.float32),
            pltpu.VMEM((mb, ny), jnp.float32),
            pltpu.VMEM((mb, ny), jnp.float32),
            pltpu.VMEM((mb, ny), jnp.float32),
            pltpu.VMEM((mb, ny), jnp.float32),
            pltpu.VMEM((mb, ny), jnp.float32),
            pltpu.VMEM((mb, ny), jnp.float32),
            pltpu.SemaphoreType.DMA((4,)),
            pltpu.SemaphoreType.DMA((sides,)),
            pltpu.SemaphoreType.DMA((sides,)),
            pltpu.SemaphoreType.DMA((sides, rows // 2 + 1)),
            pltpu.SemaphoreType.DMA((sides, 1 + len(LATE))),
            pltpu.SemaphoreType.DMA((5,)),
            pltpu.SemaphoreType.DMA((4,)),
            pltpu.SemaphoreType.DMA((2,)),
            pltpu.SemaphoreType.REGULAR,
        ],
        compiler_params=pltpu.CompilerParams(collective_id=0, has_side_effects=True, vmem_limit_bytes=24 * 2**20),
    )(*[pltpu.with_memory_space_constraint(x, pltpu.HBM)
        for x in (field, kappa_x, kappa_y, coupling, pattern)])
    tiles = out.reshape(mb, rows // 8, ny // 128, 8, 128)
    return jnp.swapaxes(tiles, 2, 3).reshape(mb, rows, ny)


def solution(mesh):
    placed = (
        P("mode", "space", None),
        P(None, "space", None),
        P(None, "space", None),
        P("mode", None, None, None),
        P("mode", None, None, None),
    )
    return jax.shard_map(
        functools.partial(shards, mesh.shape["mode"], mesh.shape["space"]),
        mesh=mesh, in_specs=placed, out_specs=P("mode", "space", None), check_vma=False)
```

```python
import functools

import jax
import jax.numpy as jnp
from jax import lax
from jax.experimental import pallas as pl
from jax.experimental.pallas import tpu as pltpu
from jax.sharding import PartitionSpec as P

LANES = 256
PART = 16
EARLY = 128
LATE = (384,)
ASIDE = 384


def kernel(n_mode, n_space, field_hbm, kx_hbm, ky_hbm, coup_hbm, pat_hbm, out_ref,
           raw, raw_in, tall, u_ext, v_ext, kappa, ky_left, coup, pat, packed, packed_in, relay, own_ref, mixed_ref, coef_ref,
           kx_in, pend, low, q_row, z_row, first_row, last_row, high,
           local_sem, field_send, early_recv, row_recv, piece_recv, other_send, other_recv, relay_sem, hello):
    mb, rows, ny = field_hbm.shape
    group = 128 // mb
    terms = kx_hbm.shape[0]
    sides = v_ext.shape[0]
    early = raw_in.shape[-1]
    mode = lax.axis_index("mode")
    space = lax.axis_index("space")
    above = {"space": lax.rem(space + 1, n_space)}
    below = {"space": lax.rem(space + n_space - 1, n_space)}
    upper = {"mode": lax.rem(mode + 1, n_mode)}
    lower = {"mode": lax.rem(mode + n_mode - 1, n_mode)}
    has_below = space > 0
    has_above = space < n_space - 1
    kx_ref, ky_ref = kappa.at[0], kappa.at[1]

    barrier = pltpu.get_barrier_semaphore()

    def greet(target):
        pl.semaphore_signal(barrier, inc=1, device_id=target, device_id_type=pl.DeviceIdType.MESH)

    for target in (upper, lower)[:sides]:
        greet(target)
    pl.when(has_above)(lambda: greet(above))

    field_load = pltpu.make_async_copy(field_hbm, raw, local_sem.at[0])
    coup_load = pltpu.make_async_copy(coup_hbm, coup, local_sem.at[1])
    pat_load = pltpu.make_async_copy(pat_hbm, pat, local_sem.at[2])
    kx_load = pltpu.make_async_copy(kx_hbm, kx_ref, local_sem.at[3])
    ky_load = pltpu.make_async_copy(ky_hbm, ky_ref, local_sem.at[3])
    for copy in (field_load, coup_load, pat_load, kx_load, ky_load):
        copy.start()

    def masked(slot, k):
        return jnp.where(pat[slot, k] > 0, coup[slot, k].astype(jnp.float32), 0.0)

    def placed(block, shape, offset, flip=False):
        spot = lax.broadcasted_iota(jnp.int32, shape, 0) + offset
        place = jnp.where(lax.broadcasted_iota(jnp.int32, shape, 1) == spot, 1.0, 0.0).astype(jnp.bfloat16)
        return lax.dot_general(block.astype(jnp.bfloat16), place, (((0 if flip else 1,), (0,)), ((), ())),
                               preferred_element_type=jnp.float32)

    def by_rows(source, target, first, count, width):
        for c in range(0, width, 128):
            tall[:mb * count] = source[:, first:first + count, c:c + 128].astype(jnp.float32).reshape(mb * count, 128)
            for r in range(count):
                target[first + r + 1, :, c:c + 128] = tall[pl.ds(r, mb, stride=count), :].astype(jnp.bfloat16)

    pl.semaphore_wait(barrier, sides + jnp.where(has_below, 1, 0))

    @pl.when(has_below)
    def _():
        pl.semaphore_signal(hello, inc=1, device_id=below, device_id_type=pl.DeviceIdType.MESH)

    def remote(src, dst, send, recv, target):
        return pltpu.make_async_remote_copy(
            src_ref=src, dst_ref=dst, send_sem=send, recv_sem=recv,
            device_id=target, device_id_type=pl.DeviceIdType.MESH)

    towards = (lower, upper)
    cuts = [early] + [ny - w for w in LATE if ny - w > early] + [ny]
    pieces = list(zip(cuts[:-1], cuts[1:]))
    pairs = (rows - 6) // 2
    rest = pl.ds(early, ny - early)

    def rows_copy(side, first, count, at, cols=rest, recv=row_recv):
        part = pl.ds(first + 1, count)
        return remote(u_ext.at[part, :, cols], v_ext.at[side, part, :, cols],
                      field_send.at[side], recv.at[side, at], towards[side])

    def pair_copy(side, h):
        return rows_copy(side, 2 * h + 3, 2, h + 4)

    def early_row(side):
        return rows_copy(side, 2, 1, 2)

    def late_row(side):
        return rows_copy(side, rows - 3, 1, 3)

    def piece_copy(side, p):
        first, last = pieces[p]
        return rows_copy(side, rows - 2, 1, p, pl.ds(first, last - first), piece_recv)

    def early_copy(side):
        return remote(field_hbm.at[:, :, pl.ds(0, early)], raw_in.at[side], field_send.at[side], early_recv.at[side], towards[side])

    def halo_up(side):
        return remote(v_ext.at[side, rows], v_ext.at[side, 0], other_send.at[1], other_recv.at[1], above)

    def halo_down(side):
        return remote(v_ext.at[side, 1], v_ext.at[side, rows + 1], other_send.at[2], other_recv.at[2], below)

    shared = n_space % 2 == 0
    sends_coup = lax.rem(space, 2) == 0 if shared else space >= 0
    coup_pass = remote(packed_in, packed_in, other_send.at[4], other_recv.at[0], above)
    coup_copy = remote(packed, packed_in, other_send.at[0], other_recv.at[0], upper)
    last_copy = remote(u_ext.at[rows], u_ext.at[0], other_send.at[1], other_recv.at[1], above)
    first_copy = remote(u_ext.at[1], u_ext.at[rows + 1], other_send.at[2], other_recv.at[2], below)
    kx_copy = remote(kx_hbm.at[:, pl.ds(rows - 8, 8), :], kx_in, other_send.at[3], other_recv.at[3], above)

    def strips(count, sem):
        part = u_ext.at[pl.ds(0, count)]
        return pltpu.make_async_copy(part, part, sem)

    for side in range(sides):
        early_copy(side).start()

    coup_load.wait()
    pat_load.wait()

    @pl.when(sends_coup)
    def _():
        for q in range(terms // group):
            beside = None
            for p in range(group):
                part = placed(masked(1, q * group + p), (mb, 128), p * mb, flip=True)
                beside = part if beside is None else beside + part
            packed[q * mb:(q + 1) * mb] = beside.astype(jnp.bfloat16)
        coup_copy.start()

    field_load.wait()
    by_rows(raw, u_ext, 0, rows, ny)
    pl.when(has_above)(lambda: pl.semaphore_wait(hello, 1))

    detours = [(1, ny - early), (3, min(ASIDE, ny - early))] if sides == 1 and n_space > 4 else []
    strong = (mode == 1) & ((space == 1) | (space == 3))
    weak = (mode == 1) & (lax.rem(space, 2) == 1) & (space > 3)
    yields = strong | weak if detours else space < 0
    hops = []
    for at, width in detours:
        part = pl.ds(early, width)
        held_part = relay.at[:, :, pl.ds(0, width)]
        hops.append((
            (mode == 1) & (space == at), (mode == 1) & (space == at + 1), (mode == 0) & (space == at + 1),
            remote(u_ext.at[pl.ds(3, 1), :, part], held_part, field_send.at[0], relay_sem.at[0], above),
            remote(held_part, held_part, relay_sem.at[1], relay_sem.at[0], upper),
            remote(held_part, v_ext.at[0, pl.ds(3, 1), :, part], relay_sem.at[1], row_recv.at[0, 2], below)))

    def early_rows(here):
        whole = here
        for (at, width), hop in zip(detours, hops):
            whole = whole & jnp.logical_not(hop[0])
            if width < ny - early:
                pl.when(here & hop[0])(rows_copy(0, 2, 1, 2, pl.ds(early + width, ny - early - width)).start)
        for side in range(sides):
            pl.when(whole)(early_row(side).start)

    for source, _, _, leave_copy, _, _ in hops:
        pl.when(source)(leave_copy.start)
    for side in range(sides):
        rows_copy(side, 0, 2, 0).start()
    pl.when(has_below)(first_copy.start)
    for _, middle, _, leave_copy, cross_copy, _ in hops:
        @pl.when(middle)
        def _():
            leave_copy.wait_recv()
            cross_copy.start()
    for side in range(sides):
        rows_copy(side, rows - 1, 1, 1).start()
    early_rows(jnp.logical_not(strong))
    for _, _, turn, _, cross_copy, come_copy in hops:
        @pl.when(turn)
        def _():
            cross_copy.wait_recv()
            come_copy.start()

    def send_rest():
        if detours:
            early_rows(strong)
        for side in range(sides):
            @pl.loop(0, pairs)
            def _(h):
                pair_copy(side, h).start()
        for side in range(sides):
            late_row(side).start()
        for p in range(len(pieces)):
            for side in range(sides):
                piece_copy(side, p).start()

        @pl.when(has_above)
        def _():
            last_copy.start()
            kx_copy.start()

    pl.when(jnp.logical_not(yields))(send_rest)

    for k in range(terms):
        half = masked(0, k) * 0.5
        shape = (mb, 4 * mb)
        coef = placed(half, shape, 0) + placed(half, shape, mb, flip=True) + placed(masked(1, k), shape, 2 * mb)
        own_ref[k * mb:(k + 1) * mb] = coef

    for side in range(sides):
        early_copy(side).wait_recv()
    for side in range(sides):
        by_rows(raw_in.at[side], v_ext.at[side], 0, rows, early)
    coup_copy.wait_recv()
    if shared:
        pl.when(sends_coup)(coup_pass.start)
    pltpu.make_async_copy(kappa, kappa, local_sem.at[3]).wait()
    for k in range(terms):
        lane = lax.broadcasted_iota(jnp.int32, (rows, ny), 1)
        ky_left[k] = jnp.where(lane == 0, 0.0, pltpu.roll(ky_ref[k], 1, axis=1))
    for k in range(terms):
        q, p = divmod(k, group)
        shape = (mb, 4 * mb)
        coef = (own_ref[k * mb:(k + 1) * mb]
                + placed(packed_in[q * mb:(q + 1) * mb, p * mb:(p + 1) * mb], shape, 3 * mb))
        for m in range(0, mb, PART):
            own_at = m * terms + k * PART
            mixed_ref[own_at:own_at + PART] = coef[m:m + PART]
    coef_ref[...] = mixed_ref[...].astype(jnp.bfloat16)
    for side in range(sides):
        rows_copy(side, 0, 2, 0).wait_recv()
        pl.when(has_below)(halo_down(side).start)
    if detours:
        pl.when(yields)(send_rest)
    for side in range(sides):
        rows_copy(side, rows - 1, 1, 1).wait_recv()
        pl.when(has_above)(halo_up(side).start)

    coef = coef_ref[...]
    final = rows - 1
    late = rows - 2

    def w_of(e, cols):
        u = u_ext[e, :, cols]
        vs = [v_ext[side, e, :, cols] for side in range(sides)]
        return jnp.dot(coef, jnp.concatenate([u, u, vs[0], vs[-1]], axis=0), preferred_element_type=jnp.float32)

    def sums(w, *weights):
        parts = [[] for _ in weights]
        scales = [[weight(k) for k in range(terms)] for weight in weights]
        for m in range(0, mb, PART):
            totals = [None] * len(weights)
            for k in range(terms):
                part = w[m * terms + k * PART:m * terms + (k + 1) * PART]
                for i in range(len(weights)):
                    value = scales[i][k] * part
                    totals[i] = value if totals[i] is None else totals[i] + value
            for i in range(len(weights)):
                parts[i].append(totals[i])
        return [jnp.concatenate(p, axis=0) for p in parts]

    def row_of(ref, r, cols):
        return lambda k: ref[k, pl.ds(r, 1), cols]

    def from_left(q):
        lane = lax.broadcasted_iota(jnp.int32, q.shape, 1)
        return jnp.where(lane == 0, 0.0, pltpu.roll(q, 1, axis=1))

    def from_right(z):
        lane = lax.broadcasted_iota(jnp.int32, z.shape, 1)
        return jnp.where(lane == z.shape[1] - 1, 0.0, pltpu.roll(z, z.shape[1] - 1, axis=1))

    blocks = [pl.ds(c, LANES) for c in range(0, ny, LANES)]

    def put(r, cols, value):
        for at in range(0, cols.size, 128):
            tile = (cols.start + at) // 128
            start = (r // 8) * 8 * (ny // 128) + tile * 8 + r % 8
            out_ref[pl.ds(start, mb, stride=rows * (ny // 128)), :] = value[:, at:at + 128]

    def row_step(r, give):
        for cols in blocks:
            a, b, q, z = sums(w_of(r + 1, cols), row_of(kx_ref, r - 1, cols), row_of(kx_ref, r, cols),
                              row_of(ky_ref, r, cols), row_of(ky_left, r, cols))
            give(cols, a)
            pend[:, cols] = a + b + q + z - low[:, cols]
            low[:, cols] = b
            q_row[:, cols] = q
            z_row[:, cols] = z
        pend[...] = pend[...] - from_left(q_row[...]) - from_right(z_row[...])

    def full_step(r):
        row_step(r, lambda cols, a: put(r - 1, cols, pend[:, cols] - a))

    def edges():
        @pl.when(has_below)
        def _():
            strips(1 + sides, other_recv.at[1]).wait()
            kx_copy.wait_recv()

        @pl.when(has_above)
        def _():
            strips(1 + sides, other_recv.at[2]).wait()

        def blank(e):
            u_ext[e] = jnp.zeros((mb, ny), jnp.bfloat16)
            for side in range(sides):
                v_ext[side, e] = jnp.zeros((mb, ny), jnp.bfloat16)

        @pl.when(jnp.logical_not(has_below))
        def _():
            blank(0)
            kx_in[...] = jnp.zeros_like(kx_in)

        @pl.when(jnp.logical_not(has_above))
        def _():
            blank(rows + 1)

        for cols in blocks:
            outer = lambda k: kx_in[k, 7:8, cols]
            put(0, cols, first_row[:, cols] + sums(w_of(1, cols), outer)[0] - sums(w_of(0, cols), outer)[0])
            a, b, q, z = sums(w_of(rows, cols), row_of(kx_ref, late, cols), row_of(kx_ref, final, cols),
                              row_of(ky_ref, final, cols), row_of(ky_left, final, cols))
            last_row[:, cols] = a + b + q + z - sums(w_of(rows + 1, cols), row_of(kx_ref, final, cols))[0]
            high[:, cols] = a
            first_row[:, cols] = q
            z_row[:, cols] = z
        last_row[...] = last_row[...] - from_left(first_row[...]) - from_right(z_row[...])

    for cols in blocks:
        b, q, z = sums(w_of(1, cols), row_of(kx_ref, 0, cols), row_of(ky_ref, 0, cols), row_of(ky_left, 0, cols))
        low[:, cols] = b
        first_row[:, cols] = b + q + z
        q_row[:, cols] = q
        z_row[:, cols] = z
    first_row[...] = first_row[...] - from_left(q_row[...]) - from_right(z_row[...])

    def take_first(cols, a):
        first_row[:, cols] = first_row[:, cols] - a

    row_step(1, take_first)

    for side in range(sides):
        early_row(side).wait_recv()
    full_step(2)

    @pl.loop(0, pairs)
    def _(h):
        pl.when(h == pairs // 2)(edges)
        for side in range(sides):
            pair_copy(side, h).wait_recv()
        full_step(2 * h + 3)
        full_step(2 * h + 4)

    for side in range(sides):
        late_row(side).wait_recv()
    full_step(rows - 3)

    high[...] = high[...] + low[...]

    for p, (first, last) in enumerate(pieces):
        first = 0 if p == 0 else first
        width = last - first
        cols = pl.ds(first, width)
        for side in range(sides):
            piece_copy(side, p).wait_recv()
        a, b, q, z = sums(w_of(late + 1, cols), row_of(kx_ref, late - 1, cols), row_of(kx_ref, late, cols),
                          row_of(ky_ref, late, cols), row_of(ky_left, late, cols))
        put(late - 1, cols, pend[:, cols] - a)
        put(final, cols, last_row[:, cols] - b)
        total = a + b + q + z - high[:, cols]
        y_first = max(first - 128, 0)
        y_last = last if last == ny else last - 128
        y_width = y_last - y_first
        if p > 0:
            before = pl.ds(y_first, 128)
            total = jnp.concatenate([low[:, before], total], axis=1)
            z = jnp.concatenate([z_row[:, before], z], axis=1)
            left = pltpu.roll(jnp.concatenate([q_row[:, y_first - 128:first], q], axis=1), 1, axis=1)[:, 128:]
        else:
            left = from_left(q)
        right = from_right(z) if last == ny else pltpu.roll(z, z.shape[1] - 1, axis=1)
        put(late, pl.ds(y_first, y_width), (total - left - right)[:, :y_width])
        if last < ny:
            after = pl.ds(y_last, 128)
            low[:, after] = total[:, y_width:]
            z_row[:, after] = z[:, y_width:]
            q_row[:, y_last - 128:last] = q[:, q.shape[1] - 256:]

    for side in range(sides):
        pltpu.make_async_copy(raw, raw, field_send.at[side]).wait()
    for _, middle, turn, _, cross_copy, _ in hops:
        pl.when(middle | turn)(cross_copy.wait_send)

    @pl.when(sends_coup)
    def _():
        coup_copy.wait_send()
        if shared:
            coup_pass.wait_send()

    @pl.when(has_above)
    def _():
        strips(1 + sides, other_send.at[1]).wait()
        kx_copy.wait_send()

    @pl.when(has_below)
    def _():
        strips(1 + sides, other_send.at[2]).wait()


def shards(n_mode, n_space, field, kappa_x, kappa_y, coupling, pattern):
    mb, rows, ny = field.shape
    terms = kappa_x.shape[0]
    sides = 1 if n_mode == 2 else 2
    vmem = pl.BlockSpec(memory_space=pltpu.VMEM)
    hbm = pl.BlockSpec(memory_space=pltpu.HBM)
    out = pl.pallas_call(
        functools.partial(kernel, n_mode, n_space),
        out_shape=jax.ShapeDtypeStruct((mb * rows * ny // 128, 128), jnp.float32),
        in_specs=[hbm] * 5,
        out_specs=vmem,
        scratch_shapes=[
            pltpu.VMEM(field.shape, jnp.bfloat16),
            pltpu.VMEM((sides, mb, rows, min(EARLY, ny // 2)), jnp.bfloat16),
            pltpu.VMEM((mb * rows, 128), jnp.float32),
            pltpu.VMEM((rows + 2, mb, ny), jnp.bfloat16),
            pltpu.VMEM((sides, rows + 2, mb, ny), jnp.bfloat16),
            pltpu.VMEM((2,) + kappa_x.shape, jnp.float32),
            pltpu.VMEM(kappa_y.shape, jnp.float32),
            pltpu.VMEM(coupling.shape, jnp.bfloat16),
            pltpu.VMEM(pattern.shape, jnp.int32),
            pltpu.VMEM((terms * mb * mb // 128, 128), jnp.bfloat16),
            pltpu.VMEM((terms * mb * mb // 128, 128), jnp.bfloat16),
            pltpu.VMEM((1, mb, ny - min(EARLY, ny // 2)), jnp.bfloat16),
            pltpu.VMEM((terms * mb, 4 * mb), jnp.float32),
            pltpu.VMEM((terms * mb, 4 * mb), jnp.float32),
            pltpu.VMEM((terms * mb, 4 * mb), jnp.bfloat16),
            pltpu.VMEM((terms, 8, ny), jnp.float32),
            pltpu.VMEM((mb, ny), jnp.float32),
            pltpu.VMEM((mb, ny), jnp.float32),
            pltpu.VMEM((mb, ny), jnp.float32),
            pltpu.VMEM((mb, ny), jnp.float32),
            pltpu.VMEM((mb, ny), jnp.float32),
            pltpu.VMEM((mb, ny), jnp.float32),
            pltpu.VMEM((mb, ny), jnp.float32),
            pltpu.SemaphoreType.DMA((4,)),
            pltpu.SemaphoreType.DMA((sides,)),
            pltpu.SemaphoreType.DMA((sides,)),
            pltpu.SemaphoreType.DMA((sides, rows // 2 + 1)),
            pltpu.SemaphoreType.DMA((sides, 1 + len(LATE))),
            pltpu.SemaphoreType.DMA((5,)),
            pltpu.SemaphoreType.DMA((4,)),
            pltpu.SemaphoreType.DMA((2,)),
            pltpu.SemaphoreType.REGULAR,
        ],
        compiler_params=pltpu.CompilerParams(collective_id=0, has_side_effects=True, vmem_limit_bytes=24 * 2**20),
    )(*[pltpu.with_memory_space_constraint(x, pltpu.HBM)
        for x in (field, kappa_x, kappa_y, coupling, pattern)])
    tiles = out.reshape(mb, rows // 8, ny // 128, 8, 128)
    return jnp.swapaxes(tiles, 2, 3).reshape(mb, rows, ny)


def solution(mesh):
    placed = (
        P("mode", "space", None),
        P(None, "space", None),
        P(None, "space", None),
        P("mode", None, None, None),
        P("mode", None, None, None),
    )
    return jax.shard_map(
        functools.partial(shards, mesh.shape["mode"], mesh.shape["space"]),
        mesh=mesh, in_specs=placed, out_specs=P("mode", "space", None), check_vma=False)
```

```python
import functools

import jax
import jax.numpy as jnp
from jax import lax
from jax.experimental import pallas as pl
from jax.experimental.pallas import tpu as pltpu
from jax.sharding import PartitionSpec as P

LANES = 256
PART = 16
EARLY = 128
LATE = 384
ASIDE = 384


def weighted_sums(w, mb, terms, *weights):
    parts = [[] for _ in weights]
    scales = [[weight(k) for k in range(terms)] for weight in weights]
    for m in range(0, mb, PART):
        totals = [None] * len(weights)
        for k in range(terms):
            part = w[m * terms + k * PART:m * terms + (k + 1) * PART]
            for i in range(len(weights)):
                value = scales[i][k] * part
                totals[i] = value if totals[i] is None else totals[i] + value
        for i in range(len(weights)):
            parts[i].append(totals[i])
    return [jnp.concatenate(p, axis=0) for p in parts]


def from_left(q):
    lane = lax.broadcasted_iota(jnp.int32, q.shape, 1)
    return jnp.where(lane == 0, 0.0, pltpu.roll(q, 1, axis=1))


def from_right(z):
    lane = lax.broadcasted_iota(jnp.int32, z.shape, 1)
    return jnp.where(lane == z.shape[1] - 1, 0.0, pltpu.roll(z, z.shape[1] - 1, axis=1))


def closing(rows, x_ref, coef_ref, ends_ref, rim_ref, scale_ref, out_ref, tail, sem):
    mb = ends_ref.shape[1]
    sides = ends_ref.shape[0] - 1
    terms, width = scale_ref.shape[1:]
    done = pl.ds(0, x_ref.shape[1] - tail.shape[1])
    left_over = pl.ds(x_ref.shape[1] - tail.shape[1], tail.shape[1])
    bulk = pltpu.make_async_copy(x_ref.at[:, done], out_ref.at[:, done], sem.at[0])
    bulk.start()
    tail[...] = x_ref[:, left_over]
    flat = tail.reshape(mb * tail.shape[1], 128)

    def put(r, first, value):
        for at in range(0, value.shape[1], 128):
            flat[pl.ds((first + at) // 16 + r % 8, mb, stride=tail.shape[1]), :] = value[:, at:at + 128]

    u, vs = ends_ref[0], [ends_ref[1 + side] for side in range(sides)]
    w = jnp.dot(coef_ref[...], jnp.concatenate([u, u, vs[0], vs[-1]], axis=0), preferred_element_type=jnp.float32)
    a, b, q, z = weighted_sums(w, mb, terms, *[lambda k, i=i: scale_ref[i, k:k + 1, :] for i in range(4)])
    put(rows - 3, 128, rim_ref[0, :, :width] - a)
    put(rows - 1, 128, rim_ref[1, :, :width] - b)
    total = jnp.concatenate([rim_ref[3, :, :128], a + b + q + z - rim_ref[2, :, :width]], axis=1)
    left = pltpu.roll(jnp.concatenate([rim_ref[3, :, 256:512], q], axis=1), 1, axis=1)[:, 128:]
    right = from_right(jnp.concatenate([rim_ref[3, :, 128:256], z], axis=1))
    put(rows - 2, 0, total - left - right)
    rest = pltpu.make_async_copy(tail, out_ref.at[:, left_over], sem.at[1])
    rest.start()
    bulk.wait()
    rest.wait()


def kernel(n_mode, n_space, field_hbm, kx_hbm, ky_hbm, coup_hbm, pat_hbm, out_ref, coef_ref, ends_ref, rim_ref, scale_ref,
           raw, raw_in, tall, u_ext, v_ext, kappa, ky_left, coup, pat, packed, packed_in, relay, own_ref, mixed_ref,
           kx_in, pend, low, q_row, z_row, first_row, last_row, high,
           local_sem, field_send, early_recv, row_recv, piece_recv, other_send, other_recv, relay_sem, hello):
    mb, rows, ny = field_hbm.shape
    group = 128 // mb
    terms = kx_hbm.shape[0]
    sides = v_ext.shape[0]
    early = raw_in.shape[-1]
    mode = lax.axis_index("mode")
    space = lax.axis_index("space")
    above = {"space": lax.rem(space + 1, n_space)}
    below = {"space": lax.rem(space + n_space - 1, n_space)}
    upper = {"mode": lax.rem(mode + 1, n_mode)}
    lower = {"mode": lax.rem(mode + n_mode - 1, n_mode)}
    has_below = space > 0
    has_above = space < n_space - 1
    kx_ref, ky_ref = kappa.at[0], kappa.at[1]

    barrier = pltpu.get_barrier_semaphore()

    def greet(target):
        pl.semaphore_signal(barrier, inc=1, device_id=target, device_id_type=pl.DeviceIdType.MESH)

    for target in (upper, lower)[:sides]:
        greet(target)
    pl.when(has_above)(lambda: greet(above))

    field_load = pltpu.make_async_copy(field_hbm, raw, local_sem.at[0])
    coup_load = pltpu.make_async_copy(coup_hbm, coup, local_sem.at[1])
    pat_load = pltpu.make_async_copy(pat_hbm, pat, local_sem.at[2])
    kx_load = pltpu.make_async_copy(kx_hbm, kx_ref, local_sem.at[3])
    ky_load = pltpu.make_async_copy(ky_hbm, ky_ref, local_sem.at[3])
    for copy in (field_load, coup_load, pat_load, kx_load, ky_load):
        copy.start()

    def masked(slot, k):
        return jnp.where(pat[slot, k] > 0, coup[slot, k].astype(jnp.float32), 0.0)

    def placed(block, shape, offset, flip=False):
        spot = lax.broadcasted_iota(jnp.int32, shape, 0) + offset
        place = jnp.where(lax.broadcasted_iota(jnp.int32, shape, 1) == spot, 1.0, 0.0).astype(jnp.bfloat16)
        return lax.dot_general(block.astype(jnp.bfloat16), place, (((0 if flip else 1,), (0,)), ((), ())),
                               preferred_element_type=jnp.float32)

    def by_rows(source, target, first, count, width):
        for c in range(0, width, 128):
            tall[:mb * count] = source[:, first:first + count, c:c + 128].astype(jnp.float32).reshape(mb * count, 128)
            for r in range(count):
                target[first + r + 1, :, c:c + 128] = tall[pl.ds(r, mb, stride=count), :].astype(jnp.bfloat16)

    pl.semaphore_wait(barrier, sides + jnp.where(has_below, 1, 0))

    @pl.when(has_below)
    def _():
        pl.semaphore_signal(hello, inc=1, device_id=below, device_id_type=pl.DeviceIdType.MESH)

    def remote(src, dst, send, recv, target):
        return pltpu.make_async_remote_copy(
            src_ref=src, dst_ref=dst, send_sem=send, recv_sem=recv,
            device_id=target, device_id_type=pl.DeviceIdType.MESH)

    towards = (lower, upper)
    split = ny - ends_ref.shape[-1]
    pieces = [(early, split), (split, ny)]
    pairs = (rows - 6) // 2
    rest = pl.ds(early, ny - early)

    def rows_copy(side, first, count, at, cols=rest, recv=row_recv):
        part = pl.ds(first + 1, count)
        return remote(u_ext.at[part, :, cols], v_ext.at[side, part, :, cols],
                      field_send.at[side], recv.at[side, at], towards[side])

    def pair_copy(side, h):
        return rows_copy(side, 2 * h + 3, 2, h + 4)

    def early_row(side):
        return rows_copy(side, 2, 1, 2)

    def late_row(side):
        return rows_copy(side, rows - 3, 1, 3)

    def piece_copy(side, p):
        first, last = pieces[p]
        return rows_copy(side, rows - 2, 1, p, pl.ds(first, last - first), piece_recv)

    def early_copy(side):
        return remote(field_hbm.at[:, :, pl.ds(0, early)], raw_in.at[side], field_send.at[side], early_recv.at[side], towards[side])

    def halo_up(side):
        return remote(v_ext.at[side, rows], v_ext.at[side, 0], other_send.at[1], other_recv.at[1], above)

    def halo_down(side):
        return remote(v_ext.at[side, 1], v_ext.at[side, rows + 1], other_send.at[2], other_recv.at[2], below)

    shared = n_space % 2 == 0
    sends_coup = lax.rem(space, 2) == 0 if shared else space >= 0
    coup_pass = remote(packed_in, packed_in, other_send.at[4], other_recv.at[0], above)
    coup_copy = remote(packed, packed_in, other_send.at[0], other_recv.at[0], upper)
    last_copy = remote(u_ext.at[rows], u_ext.at[0], other_send.at[1], other_recv.at[1], above)
    first_copy = remote(u_ext.at[1], u_ext.at[rows + 1], other_send.at[2], other_recv.at[2], below)
    kx_copy = remote(kx_hbm.at[:, pl.ds(rows - 8, 8), :], kx_in, other_send.at[3], other_recv.at[3], above)

    def strips(count, sem):
        part = u_ext.at[pl.ds(0, count)]
        return pltpu.make_async_copy(part, part, sem)

    for side in range(sides):
        early_copy(side).start()

    coup_load.wait()
    pat_load.wait()

    @pl.when(sends_coup)
    def _():
        for q in range(terms // group):
            beside = None
            for p in range(group):
                part = placed(masked(1, q * group + p), (mb, 128), p * mb, flip=True)
                beside = part if beside is None else beside + part
            packed[q * mb:(q + 1) * mb] = beside.astype(jnp.bfloat16)
        coup_copy.start()

    field_load.wait()
    by_rows(raw, u_ext, 0, rows, ny)
    pl.when(has_above)(lambda: pl.semaphore_wait(hello, 1))

    detours = [(1, ny - early), (3, min(ASIDE, ny - early))] if sides == 1 and n_space > 4 else []
    strong = (mode == 1) & ((space == 1) | (space == 3))
    weak = (mode == 1) & (lax.rem(space, 2) == 1) & (space > 3)
    yields = strong | weak if detours else space < 0
    hops = []
    for at, width in detours:
        part = pl.ds(early, width)
        held_part = relay.at[:, :, pl.ds(0, width)]
        hops.append((
            (mode == 1) & (space == at), (mode == 1) & (space == at + 1), (mode == 0) & (space == at + 1),
            remote(u_ext.at[pl.ds(3, 1), :, part], held_part, field_send.at[0], relay_sem.at[0], above),
            remote(held_part, held_part, relay_sem.at[1], relay_sem.at[0], upper),
            remote(held_part, v_ext.at[0, pl.ds(3, 1), :, part], relay_sem.at[1], row_recv.at[0, 2], below)))

    def early_rows(here):
        whole = here
        for (at, width), hop in zip(detours, hops):
            whole = whole & jnp.logical_not(hop[0])
            if width < ny - early:
                pl.when(here & hop[0])(rows_copy(0, 2, 1, 2, pl.ds(early + width, ny - early - width)).start)
        for side in range(sides):
            pl.when(whole)(early_row(side).start)

    for source, _, _, leave_copy, _, _ in hops:
        pl.when(source)(leave_copy.start)
    for side in range(sides):
        rows_copy(side, 0, 2, 0).start()
    pl.when(has_below)(first_copy.start)
    for _, middle, _, leave_copy, cross_copy, _ in hops:
        @pl.when(middle)
        def _():
            leave_copy.wait_recv()
            cross_copy.start()
    for side in range(sides):
        rows_copy(side, rows - 1, 1, 1).start()
    early_rows(jnp.logical_not(strong))
    for _, _, turn, _, cross_copy, come_copy in hops:
        @pl.when(turn)
        def _():
            cross_copy.wait_recv()
            come_copy.start()

    def send_rest():
        if detours:
            early_rows(strong)
        for side in range(sides):
            @pl.loop(0, pairs)
            def _(h):
                pair_copy(side, h).start()
        for side in range(sides):
            late_row(side).start()
        for p in range(len(pieces)):
            for side in range(sides):
                piece_copy(side, p).start()

        @pl.when(has_above)
        def _():
            last_copy.start()
            kx_copy.start()

    pl.when(jnp.logical_not(yields))(send_rest)

    for k in range(terms):
        half = masked(0, k) * 0.5
        shape = (mb, 4 * mb)
        coef = placed(half, shape, 0) + placed(half, shape, mb, flip=True) + placed(masked(1, k), shape, 2 * mb)
        own_ref[k * mb:(k + 1) * mb] = coef

    for side in range(sides):
        early_copy(side).wait_recv()
    for side in range(sides):
        by_rows(raw_in.at[side], v_ext.at[side], 0, rows, early)
    coup_copy.wait_recv()
    if shared:
        pl.when(sends_coup)(coup_pass.start)
    pltpu.make_async_copy(kappa, kappa, local_sem.at[3]).wait()
    for k in range(terms):
        lane = lax.broadcasted_iota(jnp.int32, (rows, ny), 1)
        ky_left[k] = jnp.where(lane == 0, 0.0, pltpu.roll(ky_ref[k], 1, axis=1))
    for k in range(terms):
        q, p = divmod(k, group)
        shape = (mb, 4 * mb)
        coef = (own_ref[k * mb:(k + 1) * mb]
                + placed(packed_in[q * mb:(q + 1) * mb, p * mb:(p + 1) * mb], shape, 3 * mb))
        for m in range(0, mb, PART):
            own_at = m * terms + k * PART
            mixed_ref[own_at:own_at + PART] = coef[m:m + PART]
    coef_ref[...] = mixed_ref[...].astype(jnp.bfloat16)
    for side in range(sides):
        rows_copy(side, 0, 2, 0).wait_recv()
        pl.when(has_below)(halo_down(side).start)
    if detours:
        pl.when(yields)(send_rest)
    for side in range(sides):
        rows_copy(side, rows - 1, 1, 1).wait_recv()
        pl.when(has_above)(halo_up(side).start)

    coef = coef_ref[...]
    final = rows - 1
    late = rows - 2

    def w_of(e, cols):
        u = u_ext[e, :, cols]
        vs = [v_ext[side, e, :, cols] for side in range(sides)]
        return jnp.dot(coef, jnp.concatenate([u, u, vs[0], vs[-1]], axis=0), preferred_element_type=jnp.float32)

    def sums(w, *weights):
        return weighted_sums(w, mb, terms, *weights)

    def row_of(ref, r, cols):
        return lambda k: ref[k, pl.ds(r, 1), cols]

    blocks = [pl.ds(c, LANES) for c in range(0, ny, LANES)]

    def put(r, cols, value):
        for at in range(0, cols.size, 128):
            tile = (cols.start + at) // 128
            start = (r // 8) * 8 * (ny // 128) + tile * 8 + r % 8
            out_ref[pl.ds(start, mb, stride=rows * (ny // 128)), :] = value[:, at:at + 128]

    def row_step(r, give):
        for cols in blocks:
            a, b, q, z = sums(w_of(r + 1, cols), row_of(kx_ref, r - 1, cols), row_of(kx_ref, r, cols),
                              row_of(ky_ref, r, cols), row_of(ky_left, r, cols))
            give(cols, a)
            pend[:, cols] = a + b + q + z - low[:, cols]
            low[:, cols] = b
            q_row[:, cols] = q
            z_row[:, cols] = z
        pend[...] = pend[...] - from_left(q_row[...]) - from_right(z_row[...])

    def full_step(r):
        row_step(r, lambda cols, a: put(r - 1, cols, pend[:, cols] - a))

    def edges():
        @pl.when(has_below)
        def _():
            strips(1 + sides, other_recv.at[1]).wait()
            kx_copy.wait_recv()

        @pl.when(has_above)
        def _():
            strips(1 + sides, other_recv.at[2]).wait()

        def blank(e):
            u_ext[e] = jnp.zeros((mb, ny), jnp.bfloat16)
            for side in range(sides):
                v_ext[side, e] = jnp.zeros((mb, ny), jnp.bfloat16)

        @pl.when(jnp.logical_not(has_below))
        def _():
            blank(0)
            kx_in[...] = jnp.zeros_like(kx_in)

        @pl.when(jnp.logical_not(has_above))
        def _():
            blank(rows + 1)

        for cols in blocks:
            outer = lambda k: kx_in[k, 7:8, cols]
            put(0, cols, first_row[:, cols] + sums(w_of(1, cols), outer)[0] - sums(w_of(0, cols), outer)[0])
            a, b, q, z = sums(w_of(rows, cols), row_of(kx_ref, late, cols), row_of(kx_ref, final, cols),
                              row_of(ky_ref, final, cols), row_of(ky_left, final, cols))
            last_row[:, cols] = a + b + q + z - sums(w_of(rows + 1, cols), row_of(kx_ref, final, cols))[0]
            high[:, cols] = a
            first_row[:, cols] = q
            z_row[:, cols] = z
        last_row[...] = last_row[...] - from_left(first_row[...]) - from_right(z_row[...])

    for cols in blocks:
        b, q, z = sums(w_of(1, cols), row_of(kx_ref, 0, cols), row_of(ky_ref, 0, cols), row_of(ky_left, 0, cols))
        low[:, cols] = b
        first_row[:, cols] = b + q + z
        q_row[:, cols] = q
        z_row[:, cols] = z
    first_row[...] = first_row[...] - from_left(q_row[...]) - from_right(z_row[...])

    def take_first(cols, a):
        first_row[:, cols] = first_row[:, cols] - a

    row_step(1, take_first)

    for side in range(sides):
        early_row(side).wait_recv()
    full_step(2)

    @pl.loop(0, pairs)
    def _(h):
        pl.when(h == pairs // 2)(edges)
        for side in range(sides):
            pair_copy(side, h).wait_recv()
        full_step(2 * h + 3)
        full_step(2 * h + 4)

    for side in range(sides):
        late_row(side).wait_recv()
    full_step(rows - 3)

    high[...] = high[...] + low[...]

    last = pieces[0][1]
    cols = pl.ds(0, last)
    for side in range(sides):
        piece_copy(side, 0).wait_recv()
    a, b, q, z = sums(w_of(late + 1, cols), row_of(kx_ref, late - 1, cols), row_of(kx_ref, late, cols),
                      row_of(ky_ref, late, cols), row_of(ky_left, late, cols))
    put(late - 1, cols, pend[:, cols] - a)
    put(final, cols, last_row[:, cols] - b)
    total = a + b + q + z - high[:, cols]
    right = pltpu.roll(z, last - 1, axis=1)
    put(late, pl.ds(0, last - 128), (total - from_left(q) - right)[:, :last - 128])
    rim_ref[3, :, :128] = total[:, last - 128:]
    rim_ref[3, :, 128:256] = z[:, last - 128:]
    rim_ref[3, :, 256:512] = q[:, last - 256:]
    end = pl.ds(last, ny - last)
    for i, part in enumerate((pend, last_row, high)):
        rim_ref[i, :, :ny - last] = part[:, end]
    for k in range(terms):
        for i, (part, r) in enumerate(((kx_ref, late - 1), (kx_ref, late), (ky_ref, late), (ky_left, late))):
            scale_ref[i, k:k + 1, :] = part[k, r:r + 1, end]
    ends_ref[0] = u_ext[late + 1, :, end]
    for side in range(sides):
        piece_copy(side, 1).wait_recv()
        ends_ref[1 + side] = v_ext[side, late + 1, :, end]

    for side in range(sides):
        pltpu.make_async_copy(raw, raw, field_send.at[side]).wait()
    for _, middle, turn, _, cross_copy, _ in hops:
        pl.when(middle | turn)(cross_copy.wait_send)

    @pl.when(sends_coup)
    def _():
        coup_copy.wait_send()
        if shared:
            coup_pass.wait_send()

    @pl.when(has_above)
    def _():
        strips(1 + sides, other_send.at[1]).wait()
        kx_copy.wait_send()

    @pl.when(has_below)
    def _():
        strips(1 + sides, other_send.at[2]).wait()


def shards(n_mode, n_space, field, kappa_x, kappa_y, coupling, pattern):
    mb, rows, ny = field.shape
    terms = kappa_x.shape[0]
    sides = 1 if n_mode == 2 else 2
    vmem = pl.BlockSpec(memory_space=pltpu.VMEM)
    hbm = pl.BlockSpec(memory_space=pltpu.HBM)
    across = rows * ny // 128
    width = min(LATE, ny - 512)
    results = pl.pallas_call(
        functools.partial(kernel, n_mode, n_space),
        out_shape=[
            jax.ShapeDtypeStruct((mb * across, 128), jnp.float32),
            jax.ShapeDtypeStruct((terms * mb, 4 * mb), jnp.bfloat16),
            jax.ShapeDtypeStruct((1 + sides, mb, width), jnp.bfloat16),
            jax.ShapeDtypeStruct((4, mb, 512), jnp.float32),
            jax.ShapeDtypeStruct((4, terms, width), jnp.float32),
        ],
        in_specs=[hbm] * 5,
        out_specs=[vmem] * 5,
        scratch_shapes=[
            pltpu.VMEM(field.shape, jnp.bfloat16),
            pltpu.VMEM((sides, mb, rows, min(EARLY, ny // 2)), jnp.bfloat16),
            pltpu.VMEM((mb * rows, 128), jnp.float32),
            pltpu.VMEM((rows + 2, mb, ny), jnp.bfloat16),
            pltpu.VMEM((sides, rows + 2, mb, ny), jnp.bfloat16),
            pltpu.VMEM((2,) + kappa_x.shape, jnp.float32),
            pltpu.VMEM(kappa_y.shape, jnp.float32),
            pltpu.VMEM(coupling.shape, jnp.bfloat16),
            pltpu.VMEM(pattern.shape, jnp.int32),
            pltpu.VMEM((terms * mb * mb // 128, 128), jnp.bfloat16),
            pltpu.VMEM((terms * mb * mb // 128, 128), jnp.bfloat16),
            pltpu.VMEM((1, mb, ny - min(EARLY, ny // 2)), jnp.bfloat16),
            pltpu.VMEM((terms * mb, 4 * mb), jnp.float32),
            pltpu.VMEM((terms * mb, 4 * mb), jnp.float32),
            pltpu.VMEM((terms, 8, ny), jnp.float32),
            pltpu.VMEM((mb, ny), jnp.float32),
            pltpu.VMEM((mb, ny), jnp.float32),
            pltpu.VMEM((mb, ny), jnp.float32),
            pltpu.VMEM((mb, ny), jnp.float32),
            pltpu.VMEM((mb, ny), jnp.float32),
            pltpu.VMEM((mb, ny), jnp.float32),
            pltpu.VMEM((mb, ny), jnp.float32),
            pltpu.SemaphoreType.DMA((4,)),
            pltpu.SemaphoreType.DMA((sides,)),
            pltpu.SemaphoreType.DMA((sides,)),
            pltpu.SemaphoreType.DMA((sides, rows // 2 + 1)),
            pltpu.SemaphoreType.DMA((sides, 2)),
            pltpu.SemaphoreType.DMA((5,)),
            pltpu.SemaphoreType.DMA((4,)),
            pltpu.SemaphoreType.DMA((2,)),
            pltpu.SemaphoreType.REGULAR,
        ],
        compiler_params=pltpu.CompilerParams(collective_id=0, has_side_effects=True, vmem_limit_bytes=24 * 2**20),
    )(*[pltpu.with_memory_space_constraint(x, pltpu.HBM)
        for x in (field, kappa_x, kappa_y, coupling, pattern)])
    handed = [results[0].reshape(mb, across, 128)] + list(results[1:])
    handed = [pltpu.with_memory_space_constraint(x, pltpu.VMEM) for x in handed]
    out = pl.pallas_call(
        functools.partial(closing, rows),
        out_shape=jax.ShapeDtypeStruct((mb, across, 128), jnp.float32),
        in_specs=[vmem] * 5,
        out_specs=hbm,
        scratch_shapes=[
            pltpu.VMEM((mb, (width + 128) // 16, 128), jnp.float32),
            pltpu.SemaphoreType.DMA((2,)),
        ],
        compiler_params=pltpu.CompilerParams(vmem_limit_bytes=8 * 2**20),
    )(*handed)
    tiles = out.reshape(mb, rows // 8, ny // 128, 8, 128)
    return jnp.swapaxes(tiles, 2, 3).reshape(mb, rows, ny)


def solution(mesh):
    placed = (
        P("mode", "space", None),
        P(None, "space", None),
        P(None, "space", None),
        P("mode", None, None, None),
        P("mode", None, None, None),
    )
    return jax.shard_map(
        functools.partial(shards, mesh.shape["mode"], mesh.shape["space"]),
        mesh=mesh, in_specs=placed, out_specs=P("mode", "space", None), check_vma=False)
```

```python
import functools

import jax
import jax.numpy as jnp
from jax import lax
from jax.experimental import pallas as pl
from jax.experimental.pallas import tpu as pltpu
from jax.sharding import PartitionSpec as P

LANES = 256
PART = 16
EARLY = 128
LATE = 384
ASIDE = 384


def weighted_sums(w, mb, terms, *weights):
    parts = [[] for _ in weights]
    scales = [[weight(k) for k in range(terms)] for weight in weights]
    for m in range(0, mb, PART):
        totals = [None] * len(weights)
        for k in range(terms):
            part = w[m * terms + k * PART:m * terms + (k + 1) * PART]
            for i in range(len(weights)):
                value = scales[i][k] * part
                totals[i] = value if totals[i] is None else totals[i] + value
        for i in range(len(weights)):
            parts[i].append(totals[i])
    return [jnp.concatenate(p, axis=0) for p in parts]


def from_left(q):
    lane = lax.broadcasted_iota(jnp.int32, q.shape, 1)
    return jnp.where(lane == 0, 0.0, pltpu.roll(q, 1, axis=1))


def from_right(z):
    lane = lax.broadcasted_iota(jnp.int32, z.shape, 1)
    return jnp.where(lane == z.shape[1] - 1, 0.0, pltpu.roll(z, z.shape[1] - 1, axis=1))


def closing(rows, x_ref, coef_ref, ends_ref, rim_ref, scale_ref, out_ref, tail, sem):
    mb = ends_ref.shape[1]
    sides = ends_ref.shape[0] - 1
    terms, width = scale_ref.shape[1:]
    done = pl.ds(0, x_ref.shape[1] - tail.shape[1])
    left_over = pl.ds(x_ref.shape[1] - tail.shape[1], tail.shape[1])
    bulk = pltpu.make_async_copy(x_ref.at[:, done], out_ref.at[:, done], sem.at[0])
    bulk.start()
    tail[...] = x_ref[:, left_over]
    flat = tail.reshape(mb * tail.shape[1], 128)

    def put(r, first, value):
        for at in range(0, value.shape[1], 128):
            flat[pl.ds((first + at) // 16 + r % 8, mb, stride=tail.shape[1]), :] = value[:, at:at + 128]

    u, vs = ends_ref[0], [ends_ref[1 + side] for side in range(sides)]
    w = jnp.dot(coef_ref[...], jnp.concatenate([u, u, vs[0], vs[-1]], axis=0), preferred_element_type=jnp.float32)
    a, b, q, z = weighted_sums(w, mb, terms, *[lambda k, i=i: scale_ref[i, k:k + 1, :] for i in range(4)])
    put(rows - 3, 128, rim_ref[0, :, :width] - a)
    put(rows - 1, 128, rim_ref[1, :, :width] - b)
    total = jnp.concatenate([rim_ref[3, :, :128], a + b + q + z - rim_ref[2, :, :width]], axis=1)
    left = pltpu.roll(jnp.concatenate([rim_ref[3, :, 256:512], q], axis=1), 1, axis=1)[:, 128:]
    right = from_right(jnp.concatenate([rim_ref[3, :, 128:256], z], axis=1))
    put(rows - 2, 0, total - left - right)
    rest = pltpu.make_async_copy(tail, out_ref.at[:, left_over], sem.at[1])
    rest.start()
    bulk.wait()
    rest.wait()


def kernel(n_mode, n_space, field_hbm, kx_hbm, ky_hbm, coup_hbm, pat_hbm, out_ref, coef_ref, ends_ref, rim_ref, scale_ref,
           raw, raw_in, tall, u_ext, v_ext, kappa, ky_left, coup, pat, packed, packed_in, relay, own_ref, mixed_ref,
           kx_in, pend, low, q_row, z_row, first_row, last_row, high,
           local_sem, field_send, early_recv, row_recv, piece_recv, other_send, other_recv, relay_sem, hello):
    mb, rows, ny = field_hbm.shape
    group = 128 // mb
    terms = kx_hbm.shape[0]
    sides = v_ext.shape[0]
    early = raw_in.shape[-1]
    mode = lax.axis_index("mode")
    space = lax.axis_index("space")
    above = {"space": lax.rem(space + 1, n_space)}
    below = {"space": lax.rem(space + n_space - 1, n_space)}
    upper = {"mode": lax.rem(mode + 1, n_mode)}
    lower = {"mode": lax.rem(mode + n_mode - 1, n_mode)}
    has_below = space > 0
    has_above = space < n_space - 1
    kx_ref, ky_ref = kappa.at[0], kappa.at[1]

    barrier = pltpu.get_barrier_semaphore()

    def greet(target):
        pl.semaphore_signal(barrier, inc=1, device_id=target, device_id_type=pl.DeviceIdType.MESH)

    for target in (upper, lower)[:sides]:
        greet(target)
    odd = lax.rem(space, 2) == 1
    pl.when(odd)(lambda: greet(below))
    pl.when(odd & has_above)(lambda: greet(above))
    neighbours = jnp.where(has_below, 1, 0) + jnp.where(has_above, 1, 0)

    field_load = pltpu.make_async_copy(field_hbm, raw, local_sem.at[0])
    coup_load = pltpu.make_async_copy(coup_hbm, coup, local_sem.at[1])
    pat_load = pltpu.make_async_copy(pat_hbm, pat, local_sem.at[2])
    kx_load = pltpu.make_async_copy(kx_hbm, kx_ref, local_sem.at[3])
    ky_load = pltpu.make_async_copy(ky_hbm, ky_ref, local_sem.at[3])
    for copy in (field_load, coup_load, pat_load, kx_load, ky_load):
        copy.start()

    def masked(slot, k):
        return jnp.where(pat[slot, k] > 0, coup[slot, k].astype(jnp.float32), 0.0)

    def placed(block, shape, offset, flip=False):
        spot = lax.broadcasted_iota(jnp.int32, shape, 0) + offset
        place = jnp.where(lax.broadcasted_iota(jnp.int32, shape, 1) == spot, 1.0, 0.0).astype(jnp.bfloat16)
        return lax.dot_general(block.astype(jnp.bfloat16), place, (((0 if flip else 1,), (0,)), ((), ())),
                               preferred_element_type=jnp.float32)

    def by_rows(source, target, first, count, width):
        for c in range(0, width, 128):
            tall[:mb * count] = source[:, first:first + count, c:c + 128].astype(jnp.float32).reshape(mb * count, 128)
            for r in range(count):
                target[first + r + 1, :, c:c + 128] = tall[pl.ds(r, mb, stride=count), :].astype(jnp.bfloat16)

    pl.semaphore_wait(barrier, sides + jnp.where(odd, 0, neighbours))

    def answer(target):
        pl.semaphore_signal(hello, inc=1, device_id=target, device_id_type=pl.DeviceIdType.MESH)

    def remote(src, dst, send, recv, target):
        return pltpu.make_async_remote_copy(
            src_ref=src, dst_ref=dst, send_sem=send, recv_sem=recv,
            device_id=target, device_id_type=pl.DeviceIdType.MESH)

    towards = (lower, upper)
    split = ny - ends_ref.shape[-1]
    pieces = [(early, split), (split, ny)]
    pairs = (rows - 6) // 2
    rest = pl.ds(early, ny - early)

    def rows_copy(side, first, count, at, cols=rest, recv=row_recv):
        part = pl.ds(first + 1, count)
        return remote(u_ext.at[part, :, cols], v_ext.at[side, part, :, cols],
                      field_send.at[side], recv.at[side, at], towards[side])

    def pair_copy(side, h):
        return rows_copy(side, 2 * h + 3, 2, h + 4)

    def early_row(side):
        return rows_copy(side, 2, 1, 2)

    def late_row(side):
        return rows_copy(side, rows - 3, 1, 3)

    def piece_copy(side, p):
        first, last = pieces[p]
        return rows_copy(side, rows - 2, 1, p, pl.ds(first, last - first), piece_recv)

    def early_copy(side):
        return remote(field_hbm.at[:, :, pl.ds(0, early)], raw_in.at[side], field_send.at[side], early_recv.at[side], towards[side])

    def halo_up(side):
        return remote(v_ext.at[side, rows], v_ext.at[side, 0], other_send.at[1], other_recv.at[1], above)

    def halo_down(side):
        return remote(v_ext.at[side, 1], v_ext.at[side, rows + 1], other_send.at[2], other_recv.at[2], below)

    shared = n_space % 2 == 0
    sends_coup = lax.rem(space, 2) == 0 if shared else space >= 0
    coup_pass = remote(packed_in, packed_in, other_send.at[4], other_recv.at[0], above)
    coup_copy = remote(packed, packed_in, other_send.at[0], other_recv.at[0], upper)
    last_copy = remote(u_ext.at[rows], u_ext.at[0], other_send.at[1], other_recv.at[1], above)
    first_copy = remote(u_ext.at[1], u_ext.at[rows + 1], other_send.at[2], other_recv.at[2], below)
    kx_copy = remote(kx_hbm.at[:, pl.ds(rows - 8, 8), :], kx_in, other_send.at[3], other_recv.at[3], above)

    def strips(count, sem):
        part = u_ext.at[pl.ds(0, count)]
        return pltpu.make_async_copy(part, part, sem)

    for side in range(sides):
        early_copy(side).start()
    pl.when(jnp.logical_not(odd) & has_below)(lambda: answer(below))
    pl.when(jnp.logical_not(odd) & has_above)(lambda: answer(above))

    coup_load.wait()
    pat_load.wait()

    @pl.when(sends_coup)
    def _():
        for q in range(terms // group):
            beside = None
            for p in range(group):
                part = placed(masked(1, q * group + p), (mb, 128), p * mb, flip=True)
                beside = part if beside is None else beside + part
            packed[q * mb:(q + 1) * mb] = beside.astype(jnp.bfloat16)
        coup_copy.start()

    field_load.wait()
    by_rows(raw, u_ext, 0, rows, ny)
    pl.when(odd)(lambda: pl.semaphore_wait(hello, neighbours))

    detours = [(1, ny - early), (3, min(ASIDE, ny - early))] if sides == 1 and n_space > 4 else []
    weak = odd
    yields = weak if detours else space < 0
    hops = []
    for at, width in detours:
        part = pl.ds(early, width)
        held_part = relay.at[:, :, pl.ds(0, width)]
        hops.append((
            (mode == 1) & (space == at), (mode == 1) & (space == at + 1), (mode == 0) & (space == at + 1),
            remote(u_ext.at[pl.ds(3, 1), :, part], held_part, field_send.at[0], relay_sem.at[0], above),
            remote(held_part, held_part, relay_sem.at[1], relay_sem.at[0], upper),
            remote(held_part, v_ext.at[0, pl.ds(3, 1), :, part], relay_sem.at[1], row_recv.at[0, 2], below)))

    def early_rows(here):
        whole = here
        for (at, width), hop in zip(detours, hops):
            whole = whole & jnp.logical_not(hop[0])
            if width < ny - early:
                pl.when(here & hop[0])(rows_copy(0, 2, 1, 2, pl.ds(early + width, ny - early - width)).start)
        for side in range(sides):
            pl.when(whole)(early_row(side).start)

    for source, _, _, leave_copy, _, _ in hops:
        pl.when(source)(leave_copy.start)
    for side in range(sides):
        rows_copy(side, 0, 2, 0).start()
    pl.when(has_below)(first_copy.start)
    for _, middle, _, leave_copy, cross_copy, _ in hops:
        @pl.when(middle)
        def _():
            leave_copy.wait_recv()
            cross_copy.start()
    for side in range(sides):
        rows_copy(side, rows - 1, 1, 1).start()
    early_rows(space >= 0)
    turns = space < 0
    for hop in hops:
        turns = turns | hop[2]

    def send_rest():
        for side in range(sides):
            @pl.loop(0, pairs)
            def _(h):
                pair_copy(side, h).start()
        for side in range(sides):
            late_row(side).start()
        for p in range(len(pieces)):
            for side in range(sides):
                piece_copy(side, p).start()

        @pl.when(has_above)
        def _():
            last_copy.start()
            kx_copy.start()

    pl.when(jnp.logical_not(yields | turns))(send_rest)

    for k in range(terms):
        half = masked(0, k) * 0.5
        shape = (mb, 4 * mb)
        coef = placed(half, shape, 0) + placed(half, shape, mb, flip=True) + placed(masked(1, k), shape, 2 * mb)
        own_ref[k * mb:(k + 1) * mb] = coef

    for side in range(sides):
        early_copy(side).wait_recv()
    for side in range(sides):
        by_rows(raw_in.at[side], v_ext.at[side], 0, rows, early)
    coup_copy.wait_recv()
    if shared:
        pl.when(sends_coup)(coup_pass.start)
    pltpu.make_async_copy(kappa, kappa, local_sem.at[3]).wait()
    for k in range(terms):
        lane = lax.broadcasted_iota(jnp.int32, (rows, ny), 1)
        ky_left[k] = jnp.where(lane == 0, 0.0, pltpu.roll(ky_ref[k], 1, axis=1))
    for k in range(terms):
        q, p = divmod(k, group)
        shape = (mb, 4 * mb)
        coef = (own_ref[k * mb:(k + 1) * mb]
                + placed(packed_in[q * mb:(q + 1) * mb, p * mb:(p + 1) * mb], shape, 3 * mb))
        for m in range(0, mb, PART):
            own_at = m * terms + k * PART
            mixed_ref[own_at:own_at + PART] = coef[m:m + PART]
    coef_ref[...] = mixed_ref[...].astype(jnp.bfloat16)
    for side in range(sides):
        rows_copy(side, 0, 2, 0).wait_recv()
        pl.when(has_below)(halo_down(side).start)
    for _, _, turn, _, cross_copy, come_copy in hops:
        @pl.when(turn)
        def _():
            cross_copy.wait_recv()
            come_copy.start()
    if detours:
        pl.when(yields | turns)(send_rest)
    for side in range(sides):
        rows_copy(side, rows - 1, 1, 1).wait_recv()
        pl.when(has_above)(halo_up(side).start)

    coef = coef_ref[...]
    final = rows - 1
    late = rows - 2

    def w_of(e, cols):
        u = u_ext[e, :, cols]
        vs = [v_ext[side, e, :, cols] for side in range(sides)]
        return jnp.dot(coef, jnp.concatenate([u, u, vs[0], vs[-1]], axis=0), preferred_element_type=jnp.float32)

    def sums(w, *weights):
        return weighted_sums(w, mb, terms, *weights)

    def row_of(ref, r, cols):
        return lambda k: ref[k, pl.ds(r, 1), cols]

    blocks = [pl.ds(c, LANES) for c in range(0, ny, LANES)]

    def put(r, cols, value):
        for at in range(0, cols.size, 128):
            tile = (cols.start + at) // 128
            start = (r // 8) * 8 * (ny // 128) + tile * 8 + r % 8
            out_ref[pl.ds(start, mb, stride=rows * (ny // 128)), :] = value[:, at:at + 128]

    def row_step(r, give):
        for cols in blocks:
            a, b, q, z = sums(w_of(r + 1, cols), row_of(kx_ref, r - 1, cols), row_of(kx_ref, r, cols),
                              row_of(ky_ref, r, cols), row_of(ky_left, r, cols))
            give(cols, a)
            pend[:, cols] = a + b + q + z - low[:, cols]
            low[:, cols] = b
            q_row[:, cols] = q
            z_row[:, cols] = z
        pend[...] = pend[...] - from_left(q_row[...]) - from_right(z_row[...])

    def full_step(r):
        row_step(r, lambda cols, a: put(r - 1, cols, pend[:, cols] - a))

    def edges():
        @pl.when(has_below)
        def _():
            strips(1 + sides, other_recv.at[1]).wait()
            kx_copy.wait_recv()

        @pl.when(has_above)
        def _():
            strips(1 + sides, other_recv.at[2]).wait()

        def blank(e):
            u_ext[e] = jnp.zeros((mb, ny), jnp.bfloat16)
            for side in range(sides):
                v_ext[side, e] = jnp.zeros((mb, ny), jnp.bfloat16)

        @pl.when(jnp.logical_not(has_below))
        def _():
            blank(0)
            kx_in[...] = jnp.zeros_like(kx_in)

        @pl.when(jnp.logical_not(has_above))
        def _():
            blank(rows + 1)

        for cols in blocks:
            outer = lambda k: kx_in[k, 7:8, cols]
            put(0, cols, first_row[:, cols] + sums(w_of(1, cols), outer)[0] - sums(w_of(0, cols), outer)[0])
            a, b, q, z = sums(w_of(rows, cols), row_of(kx_ref, late, cols), row_of(kx_ref, final, cols),
                              row_of(ky_ref, final, cols), row_of(ky_left, final, cols))
            last_row[:, cols] = a + b + q + z - sums(w_of(rows + 1, cols), row_of(kx_ref, final, cols))[0]
            high[:, cols] = a
            first_row[:, cols] = q
            z_row[:, cols] = z
        last_row[...] = last_row[...] - from_left(first_row[...]) - from_right(z_row[...])

    for cols in blocks:
        b, q, z = sums(w_of(1, cols), row_of(kx_ref, 0, cols), row_of(ky_ref, 0, cols), row_of(ky_left, 0, cols))
        low[:, cols] = b
        first_row[:, cols] = b + q + z
        q_row[:, cols] = q
        z_row[:, cols] = z
    first_row[...] = first_row[...] - from_left(q_row[...]) - from_right(z_row[...])

    def take_first(cols, a):
        first_row[:, cols] = first_row[:, cols] - a

    row_step(1, take_first)

    for side in range(sides):
        early_row(side).wait_recv()
    full_step(2)

    @pl.loop(0, pairs)
    def _(h):
        pl.when(h == pairs // 2)(edges)
        for side in range(sides):
            pair_copy(side, h).wait_recv()
        full_step(2 * h + 3)
        full_step(2 * h + 4)

    for side in range(sides):
        late_row(side).wait_recv()
    full_step(rows - 3)

    high[...] = high[...] + low[...]

    last = pieces[0][1]
    cols = pl.ds(0, last)
    for side in range(sides):
        piece_copy(side, 0).wait_recv()
    a, b, q, z = sums(w_of(late + 1, cols), row_of(kx_ref, late - 1, cols), row_of(kx_ref, late, cols),
                      row_of(ky_ref, late, cols), row_of(ky_left, late, cols))
    put(late - 1, cols, pend[:, cols] - a)
    put(final, cols, last_row[:, cols] - b)
    total = a + b + q + z - high[:, cols]
    right = pltpu.roll(z, last - 1, axis=1)
    put(late, pl.ds(0, last - 128), (total - from_left(q) - right)[:, :last - 128])
    rim_ref[3, :, :128] = total[:, last - 128:]
    rim_ref[3, :, 128:256] = z[:, last - 128:]
    rim_ref[3, :, 256:512] = q[:, last - 256:]
    end = pl.ds(last, ny - last)
    for i, part in enumerate((pend, last_row, high)):
        rim_ref[i, :, :ny - last] = part[:, end]
    for k in range(terms):
        for i, (part, r) in enumerate(((kx_ref, late - 1), (kx_ref, late), (ky_ref, late), (ky_left, late))):
            scale_ref[i, k:k + 1, :] = part[k, r:r + 1, end]
    ends_ref[0] = u_ext[late + 1, :, end]
    for side in range(sides):
        piece_copy(side, 1).wait_recv()
        ends_ref[1 + side] = v_ext[side, late + 1, :, end]

    for side in range(sides):
        pltpu.make_async_copy(raw, raw, field_send.at[side]).wait()
    for _, middle, turn, _, cross_copy, _ in hops:
        pl.when(middle | turn)(cross_copy.wait_send)

    @pl.when(sends_coup)
    def _():
        coup_copy.wait_send()
        if shared:
            coup_pass.wait_send()

    @pl.when(has_above)
    def _():
        strips(1 + sides, other_send.at[1]).wait()
        kx_copy.wait_send()

    @pl.when(has_below)
    def _():
        strips(1 + sides, other_send.at[2]).wait()


def shards(n_mode, n_space, field, kappa_x, kappa_y, coupling, pattern):
    mb, rows, ny = field.shape
    terms = kappa_x.shape[0]
    sides = 1 if n_mode == 2 else 2
    vmem = pl.BlockSpec(memory_space=pltpu.VMEM)
    hbm = pl.BlockSpec(memory_space=pltpu.HBM)
    across = rows * ny // 128
    width = min(LATE, ny - 512)
    results = pl.pallas_call(
        functools.partial(kernel, n_mode, n_space),
        out_shape=[
            jax.ShapeDtypeStruct((mb * across, 128), jnp.float32),
            jax.ShapeDtypeStruct((terms * mb, 4 * mb), jnp.bfloat16),
            jax.ShapeDtypeStruct((1 + sides, mb, width), jnp.bfloat16),
            jax.ShapeDtypeStruct((4, mb, 512), jnp.float32),
            jax.ShapeDtypeStruct((4, terms, width), jnp.float32),
        ],
        in_specs=[hbm] * 5,
        out_specs=[vmem] * 5,
        scratch_shapes=[
            pltpu.VMEM(field.shape, jnp.bfloat16),
            pltpu.VMEM((sides, mb, rows, min(EARLY, ny // 2)), jnp.bfloat16),
            pltpu.VMEM((mb * rows, 128), jnp.float32),
            pltpu.VMEM((rows + 2, mb, ny), jnp.bfloat16),
            pltpu.VMEM((sides, rows + 2, mb, ny), jnp.bfloat16),
            pltpu.VMEM((2,) + kappa_x.shape, jnp.float32),
            pltpu.VMEM(kappa_y.shape, jnp.float32),
            pltpu.VMEM(coupling.shape, jnp.bfloat16),
            pltpu.VMEM(pattern.shape, jnp.int32),
            pltpu.VMEM((terms * mb * mb // 128, 128), jnp.bfloat16),
            pltpu.VMEM((terms * mb * mb // 128, 128), jnp.bfloat16),
            pltpu.VMEM((1, mb, ny - min(EARLY, ny // 2)), jnp.bfloat16),
            pltpu.VMEM((terms * mb, 4 * mb), jnp.float32),
            pltpu.VMEM((terms * mb, 4 * mb), jnp.float32),
            pltpu.VMEM((terms, 8, ny), jnp.float32),
            pltpu.VMEM((mb, ny), jnp.float32),
            pltpu.VMEM((mb, ny), jnp.float32),
            pltpu.VMEM((mb, ny), jnp.float32),
            pltpu.VMEM((mb, ny), jnp.float32),
            pltpu.VMEM((mb, ny), jnp.float32),
            pltpu.VMEM((mb, ny), jnp.float32),
            pltpu.VMEM((mb, ny), jnp.float32),
            pltpu.SemaphoreType.DMA((4,)),
            pltpu.SemaphoreType.DMA((sides,)),
            pltpu.SemaphoreType.DMA((sides,)),
            pltpu.SemaphoreType.DMA((sides, rows // 2 + 1)),
            pltpu.SemaphoreType.DMA((sides, 2)),
            pltpu.SemaphoreType.DMA((5,)),
            pltpu.SemaphoreType.DMA((4,)),
            pltpu.SemaphoreType.DMA((2,)),
            pltpu.SemaphoreType.REGULAR,
        ],
        compiler_params=pltpu.CompilerParams(collective_id=0, has_side_effects=True, vmem_limit_bytes=24 * 2**20),
    )(*[pltpu.with_memory_space_constraint(x, pltpu.HBM)
        for x in (field, kappa_x, kappa_y, coupling, pattern)])
    handed = [results[0].reshape(mb, across, 128)] + list(results[1:])
    handed = [pltpu.with_memory_space_constraint(x, pltpu.VMEM) for x in handed]
    out = pl.pallas_call(
        functools.partial(closing, rows),
        out_shape=jax.ShapeDtypeStruct((mb, across, 128), jnp.float32),
        in_specs=[vmem] * 5,
        out_specs=hbm,
        scratch_shapes=[
            pltpu.VMEM((mb, (width + 128) // 16, 128), jnp.float32),
            pltpu.SemaphoreType.DMA((2,)),
        ],
        compiler_params=pltpu.CompilerParams(vmem_limit_bytes=8 * 2**20),
    )(*handed)
    tiles = out.reshape(mb, rows // 8, ny // 128, 8, 128)
    return jnp.swapaxes(tiles, 2, 3).reshape(mb, rows, ny)


def solution(mesh):
    placed = (
        P("mode", "space", None),
        P(None, "space", None),
        P(None, "space", None),
        P("mode", None, None, None),
        P("mode", None, None, None),
    )
    return jax.shard_map(
        functools.partial(shards, mesh.shape["mode"], mesh.shape["space"]),
        mesh=mesh, in_specs=placed, out_specs=P("mode", "space", None), check_vma=False)
```

```python
import functools

import jax
import jax.numpy as jnp
from jax import lax
from jax.experimental import pallas as pl
from jax.experimental.pallas import tpu as pltpu
from jax.sharding import PartitionSpec as P

LANES = 256
PART = 16
EARLY = 128
LATE = 384
ASIDE = 384


def weighted_sums(w, mb, terms, *weights):
    parts = [[] for _ in weights]
    scales = [[weight(k) for k in range(terms)] for weight in weights]
    for m in range(0, mb, PART):
        totals = [None] * len(weights)
        for k in range(terms):
            part = w[m * terms + k * PART:m * terms + (k + 1) * PART]
            for i in range(len(weights)):
                value = scales[i][k] * part
                totals[i] = value if totals[i] is None else totals[i] + value
        for i in range(len(weights)):
            parts[i].append(totals[i])
    return [jnp.concatenate(p, axis=0) for p in parts]


def from_left(q):
    lane = lax.broadcasted_iota(jnp.int32, q.shape, 1)
    return jnp.where(lane == 0, 0.0, pltpu.roll(q, 1, axis=1))


def from_right(z):
    lane = lax.broadcasted_iota(jnp.int32, z.shape, 1)
    return jnp.where(lane == z.shape[1] - 1, 0.0, pltpu.roll(z, z.shape[1] - 1, axis=1))


def closing(rows, x_ref, coef_ref, ends_ref, rim_ref, scale_ref, out_ref, tail, sem):
    mb = ends_ref.shape[1]
    sides = ends_ref.shape[0] - 1
    terms, width = scale_ref.shape[1:]
    done = pl.ds(0, x_ref.shape[1] - tail.shape[1])
    left_over = pl.ds(x_ref.shape[1] - tail.shape[1], tail.shape[1])
    bulk = pltpu.make_async_copy(x_ref.at[:, done], out_ref.at[:, done], sem.at[0])
    bulk.start()
    tail[...] = x_ref[:, left_over]
    flat = tail.reshape(mb * tail.shape[1], 128)

    def put(r, first, value):
        for at in range(0, value.shape[1], 128):
            flat[pl.ds((first + at) // 16 + r % 8, mb, stride=tail.shape[1]), :] = value[:, at:at + 128]

    u, vs = ends_ref[0], [ends_ref[1 + side] for side in range(sides)]
    w = jnp.dot(coef_ref[...], jnp.concatenate([u, u, vs[0], vs[-1]], axis=0), preferred_element_type=jnp.float32)
    a, b, q, z = weighted_sums(w, mb, terms, *[lambda k, i=i: scale_ref[i, k:k + 1, :] for i in range(4)])
    put(rows - 3, 128, rim_ref[0, :, :width] - a)
    put(rows - 1, 128, rim_ref[1, :, :width] - b)
    total = jnp.concatenate([rim_ref[3, :, :128], a + b + q + z - rim_ref[2, :, :width]], axis=1)
    left = pltpu.roll(jnp.concatenate([rim_ref[3, :, 256:512], q], axis=1), 1, axis=1)[:, 128:]
    right = from_right(jnp.concatenate([rim_ref[3, :, 128:256], z], axis=1))
    put(rows - 2, 0, total - left - right)
    rest = pltpu.make_async_copy(tail, out_ref.at[:, left_over], sem.at[1])
    rest.start()
    bulk.wait()
    rest.wait()


def kernel(n_mode, n_space, field_hbm, kx_hbm, ky_hbm, coup_hbm, pat_hbm, out_ref, coef_ref, ends_ref, rim_ref, scale_ref,
           raw, raw_in, tall, u_ext, v_ext, kappa, ky_left, coup, pat, packed, packed_in, relay, own_ref, mixed_ref,
           kx_in, pend, low, q_row, z_row, first_row, last_row, high,
           local_sem, field_send, early_recv, row_recv, piece_recv, other_send, other_recv, relay_sem, hello):
    mb, rows, ny = field_hbm.shape
    group = 128 // mb
    terms = kx_hbm.shape[0]
    sides = v_ext.shape[0]
    early = raw_in.shape[-1]
    mode = lax.axis_index("mode")
    space = lax.axis_index("space")
    above = {"space": lax.rem(space + 1, n_space)}
    below = {"space": lax.rem(space + n_space - 1, n_space)}
    upper = {"mode": lax.rem(mode + 1, n_mode)}
    lower = {"mode": lax.rem(mode + n_mode - 1, n_mode)}
    has_below = space > 0
    has_above = space < n_space - 1
    kx_ref, ky_ref = kappa.at[0], kappa.at[1]

    barrier = pltpu.get_barrier_semaphore()

    def greet(target):
        pl.semaphore_signal(barrier, inc=1, device_id=target, device_id_type=pl.DeviceIdType.MESH)

    for target in (upper, lower)[:sides]:
        greet(target)
    odd = lax.rem(space, 2) == 1
    pl.when(odd)(lambda: greet(below))
    pl.when(odd & has_above)(lambda: greet(above))
    neighbours = jnp.where(has_below, 1, 0) + jnp.where(has_above, 1, 0)

    field_load = pltpu.make_async_copy(field_hbm, raw, local_sem.at[0])
    coup_load = pltpu.make_async_copy(coup_hbm, coup, local_sem.at[1])
    pat_load = pltpu.make_async_copy(pat_hbm, pat, local_sem.at[2])
    kx_load = pltpu.make_async_copy(kx_hbm, kx_ref, local_sem.at[3])
    ky_load = pltpu.make_async_copy(ky_hbm, ky_ref, local_sem.at[3])
    for copy in (field_load, coup_load, pat_load, kx_load, ky_load):
        copy.start()

    def masked(slot, k):
        return jnp.where(pat[slot, k] > 0, coup[slot, k].astype(jnp.float32), 0.0)

    def placed(block, shape, offset, flip=False):
        spot = lax.broadcasted_iota(jnp.int32, shape, 0) + offset
        place = jnp.where(lax.broadcasted_iota(jnp.int32, shape, 1) == spot, 1.0, 0.0).astype(jnp.bfloat16)
        return lax.dot_general(block.astype(jnp.bfloat16), place, (((0 if flip else 1,), (0,)), ((), ())),
                               preferred_element_type=jnp.float32)

    def by_rows(source, target, first, count, width):
        for c in range(0, width, 128):
            tall[:mb * count] = source[:, first:first + count, c:c + 128].astype(jnp.float32).reshape(mb * count, 128)
            for r in range(count):
                target[first + r + 1, :, c:c + 128] = tall[pl.ds(r, mb, stride=count), :].astype(jnp.bfloat16)

    pl.semaphore_wait(barrier, sides + jnp.where(odd, 0, neighbours))

    def answer(target):
        pl.semaphore_signal(hello, inc=1, device_id=target, device_id_type=pl.DeviceIdType.MESH)

    def remote(src, dst, send, recv, target):
        return pltpu.make_async_remote_copy(
            src_ref=src, dst_ref=dst, send_sem=send, recv_sem=recv,
            device_id=target, device_id_type=pl.DeviceIdType.MESH)

    towards = (lower, upper)
    split = ny - ends_ref.shape[-1]
    pieces = [(early, split), (split, ny)]
    pairs = (rows - 6) // 2
    rest = pl.ds(early, ny - early)

    def rows_copy(side, first, count, at, cols=rest, recv=row_recv):
        part = pl.ds(first + 1, count)
        return remote(u_ext.at[part, :, cols], v_ext.at[side, part, :, cols],
                      field_send.at[side], recv.at[side, at], towards[side])

    def pair_copy(side, h):
        return rows_copy(side, 2 * h + 3, 2, h + 4)

    def early_row(side):
        return rows_copy(side, 2, 1, 2)

    def late_row(side):
        return rows_copy(side, rows - 3, 1, 3)

    def piece_copy(side, p):
        first, last = pieces[p]
        return rows_copy(side, rows - 2, 1, p, pl.ds(first, last - first), piece_recv)

    def early_copy(side):
        return remote(field_hbm.at[:, :, pl.ds(0, early)], raw_in.at[side], field_send.at[side], early_recv.at[side], towards[side])

    def halo_up(side):
        return remote(v_ext.at[side, rows], v_ext.at[side, 0], other_send.at[1], other_recv.at[1], above)

    def halo_down(side):
        return remote(v_ext.at[side, 1], v_ext.at[side, rows + 1], other_send.at[2], other_recv.at[2], below)

    shared = n_space % 2 == 0
    sends_coup = lax.rem(space, 2) == 0 if shared else space >= 0
    coup_pass = remote(packed_in, packed_in, other_send.at[4], other_recv.at[0], above)
    coup_copy = remote(packed, packed_in, other_send.at[0], other_recv.at[0], upper)
    last_copy = remote(u_ext.at[rows], u_ext.at[0], other_send.at[1], other_recv.at[1], above)
    first_copy = remote(u_ext.at[1], u_ext.at[rows + 1], other_send.at[2], other_recv.at[2], below)
    kx_copy = remote(kx_hbm.at[:, pl.ds(rows - 8, 8), :], kx_in, other_send.at[3], other_recv.at[3], above)

    def strips(count, sem):
        part = u_ext.at[pl.ds(0, count)]
        return pltpu.make_async_copy(part, part, sem)

    for side in range(sides):
        early_copy(side).start()
    pl.when(jnp.logical_not(odd) & has_below)(lambda: answer(below))
    pl.when(jnp.logical_not(odd) & has_above)(lambda: answer(above))

    coup_load.wait()
    pat_load.wait()

    @pl.when(sends_coup)
    def _():
        for q in range(terms // group):
            beside = None
            for p in range(group):
                part = placed(masked(1, q * group + p), (mb, 128), p * mb, flip=True)
                beside = part if beside is None else beside + part
            packed[q * mb:(q + 1) * mb] = beside.astype(jnp.bfloat16)
        coup_copy.start()

    field_load.wait()
    by_rows(raw, u_ext, 0, rows, ny)
    pl.when(odd)(lambda: pl.semaphore_wait(hello, neighbours))

    detours = [(1, ny - early), (3, min(ASIDE, ny - early))] if sides == 1 and n_space > 4 else []
    weak = odd
    yields = weak if detours else space < 0
    late_yield = odd & (mode == 0) if detours else space < 0
    hops = []
    for at, width in detours:
        part = pl.ds(early, width)
        held_part = relay.at[:, :, pl.ds(0, width)]
        hops.append((
            (mode == 1) & (space == at), (mode == 1) & (space == at + 1), (mode == 0) & (space == at + 1),
            remote(u_ext.at[pl.ds(3, 1), :, part], held_part, field_send.at[0], relay_sem.at[0], above),
            remote(held_part, held_part, relay_sem.at[1], relay_sem.at[0], upper),
            remote(held_part, v_ext.at[0, pl.ds(3, 1), :, part], relay_sem.at[1], row_recv.at[0, 2], below)))

    def early_rows(here):
        whole = here
        for (at, width), hop in zip(detours, hops):
            whole = whole & jnp.logical_not(hop[0])
            if width < ny - early:
                pl.when(here & hop[0])(rows_copy(0, 2, 1, 2, pl.ds(early + width, ny - early - width)).start)
        for side in range(sides):
            pl.when(whole)(early_row(side).start)

    for source, _, _, leave_copy, _, _ in hops:
        pl.when(source)(leave_copy.start)
    for side in range(sides):
        rows_copy(side, 0, 2, 0).start()
    pl.when(has_below)(first_copy.start)
    for _, middle, _, leave_copy, cross_copy, _ in hops:
        @pl.when(middle)
        def _():
            leave_copy.wait_recv()
            cross_copy.start()
    for side in range(sides):
        rows_copy(side, rows - 1, 1, 1).start()
    early_rows(jnp.logical_not(late_yield))
    turns = space < 0
    for hop in hops:
        turns = turns | hop[2]

    if detours:
        pl.when(turns)(pair_copy(0, 0).start)

    def send_rest():
        if detours:
            early_rows(late_yield)
        for side in range(sides):
            @pl.loop(jnp.where(turns, 1, 0), pairs)
            def _(h):
                pair_copy(side, h).start()
        for side in range(sides):
            late_row(side).start()
        for p in range(len(pieces)):
            for side in range(sides):
                piece_copy(side, p).start()

        @pl.when(has_above)
        def _():
            last_copy.start()
            kx_copy.start()

    pl.when(jnp.logical_not(yields | turns))(send_rest)

    for k in range(terms):
        half = masked(0, k) * 0.5
        shape = (mb, 4 * mb)
        coef = placed(half, shape, 0) + placed(half, shape, mb, flip=True) + placed(masked(1, k), shape, 2 * mb)
        own_ref[k * mb:(k + 1) * mb] = coef

    for side in range(sides):
        early_copy(side).wait_recv()
    for side in range(sides):
        by_rows(raw_in.at[side], v_ext.at[side], 0, rows, early)
    coup_copy.wait_recv()
    if shared:
        pl.when(sends_coup)(coup_pass.start)
    pltpu.make_async_copy(kappa, kappa, local_sem.at[3]).wait()
    for k in range(terms):
        lane = lax.broadcasted_iota(jnp.int32, (rows, ny), 1)
        ky_left[k] = jnp.where(lane == 0, 0.0, pltpu.roll(ky_ref[k], 1, axis=1))
    for k in range(terms):
        q, p = divmod(k, group)
        shape = (mb, 4 * mb)
        coef = (own_ref[k * mb:(k + 1) * mb]
                + placed(packed_in[q * mb:(q + 1) * mb, p * mb:(p + 1) * mb], shape, 3 * mb))
        for m in range(0, mb, PART):
            own_at = m * terms + k * PART
            mixed_ref[own_at:own_at + PART] = coef[m:m + PART]
    coef_ref[...] = mixed_ref[...].astype(jnp.bfloat16)
    for side in range(sides):
        rows_copy(side, 0, 2, 0).wait_recv()
        pl.when(has_below)(halo_down(side).start)
    for _, _, turn, _, cross_copy, come_copy in hops:
        @pl.when(turn)
        def _():
            cross_copy.wait_recv()
            come_copy.start()
    if detours:
        pl.when(yields | turns)(send_rest)
    for side in range(sides):
        rows_copy(side, rows - 1, 1, 1).wait_recv()
        pl.when(has_above)(halo_up(side).start)

    coef = coef_ref[...]
    final = rows - 1
    late = rows - 2

    def w_of(e, cols):
        u = u_ext[e, :, cols]
        vs = [v_ext[side, e, :, cols] for side in range(sides)]
        return jnp.dot(coef, jnp.concatenate([u, u, vs[0], vs[-1]], axis=0), preferred_element_type=jnp.float32)

    def sums(w, *weights):
        return weighted_sums(w, mb, terms, *weights)

    def row_of(ref, r, cols):
        return lambda k: ref[k, pl.ds(r, 1), cols]

    blocks = [pl.ds(c, LANES) for c in range(0, ny, LANES)]

    def put(r, cols, value):
        for at in range(0, cols.size, 128):
            tile = (cols.start + at) // 128
            start = (r // 8) * 8 * (ny // 128) + tile * 8 + r % 8
            out_ref[pl.ds(start, mb, stride=rows * (ny // 128)), :] = value[:, at:at + 128]

    def row_step(r, give):
        for cols in blocks:
            a, b, q, z = sums(w_of(r + 1, cols), row_of(kx_ref, r - 1, cols), row_of(kx_ref, r, cols),
                              row_of(ky_ref, r, cols), row_of(ky_left, r, cols))
            give(cols, a)
            pend[:, cols] = a + b + q + z - low[:, cols]
            low[:, cols] = b
            q_row[:, cols] = q
            z_row[:, cols] = z
        pend[...] = pend[...] - from_left(q_row[...]) - from_right(z_row[...])

    def full_step(r):
        row_step(r, lambda cols, a: put(r - 1, cols, pend[:, cols] - a))

    def edges():
        @pl.when(has_below)
        def _():
            strips(1 + sides, other_recv.at[1]).wait()
            kx_copy.wait_recv()

        @pl.when(has_above)
        def _():
            strips(1 + sides, other_recv.at[2]).wait()

        def blank(e):
            u_ext[e] = jnp.zeros((mb, ny), jnp.bfloat16)
            for side in range(sides):
                v_ext[side, e] = jnp.zeros((mb, ny), jnp.bfloat16)

        @pl.when(jnp.logical_not(has_below))
        def _():
            blank(0)
            kx_in[...] = jnp.zeros_like(kx_in)

        @pl.when(jnp.logical_not(has_above))
        def _():
            blank(rows + 1)

        for cols in blocks:
            outer = lambda k: kx_in[k, 7:8, cols]
            put(0, cols, first_row[:, cols] + sums(w_of(1, cols), outer)[0] - sums(w_of(0, cols), outer)[0])
            a, b, q, z = sums(w_of(rows, cols), row_of(kx_ref, late, cols), row_of(kx_ref, final, cols),
                              row_of(ky_ref, final, cols), row_of(ky_left, final, cols))
            last_row[:, cols] = a + b + q + z - sums(w_of(rows + 1, cols), row_of(kx_ref, final, cols))[0]
            high[:, cols] = a
            first_row[:, cols] = q
            z_row[:, cols] = z
        last_row[...] = last_row[...] - from_left(first_row[...]) - from_right(z_row[...])

    for cols in blocks:
        b, q, z = sums(w_of(1, cols), row_of(kx_ref, 0, cols), row_of(ky_ref, 0, cols), row_of(ky_left, 0, cols))
        low[:, cols] = b
        first_row[:, cols] = b + q + z
        q_row[:, cols] = q
        z_row[:, cols] = z
    first_row[...] = first_row[...] - from_left(q_row[...]) - from_right(z_row[...])

    def take_first(cols, a):
        first_row[:, cols] = first_row[:, cols] - a

    row_step(1, take_first)

    for side in range(sides):
        early_row(side).wait_recv()
    full_step(2)

    @pl.loop(0, pairs)
    def _(h):
        pl.when(h == pairs // 2)(edges)
        for side in range(sides):
            pair_copy(side, h).wait_recv()
        full_step(2 * h + 3)
        full_step(2 * h + 4)

    for side in range(sides):
        late_row(side).wait_recv()
    full_step(rows - 3)

    high[...] = high[...] + low[...]

    last = pieces[0][1]
    cols = pl.ds(0, last)
    for side in range(sides):
        piece_copy(side, 0).wait_recv()
    a, b, q, z = sums(w_of(late + 1, cols), row_of(kx_ref, late - 1, cols), row_of(kx_ref, late, cols),
                      row_of(ky_ref, late, cols), row_of(ky_left, late, cols))
    put(late - 1, cols, pend[:, cols] - a)
    put(final, cols, last_row[:, cols] - b)
    total = a + b + q + z - high[:, cols]
    right = pltpu.roll(z, last - 1, axis=1)
    put(late, pl.ds(0, last - 128), (total - from_left(q) - right)[:, :last - 128])
    rim_ref[3, :, :128] = total[:, last - 128:]
    rim_ref[3, :, 128:256] = z[:, last - 128:]
    rim_ref[3, :, 256:512] = q[:, last - 256:]
    end = pl.ds(last, ny - last)
    for i, part in enumerate((pend, last_row, high)):
        rim_ref[i, :, :ny - last] = part[:, end]
    for k in range(terms):
        for i, (part, r) in enumerate(((kx_ref, late - 1), (kx_ref, late), (ky_ref, late), (ky_left, late))):
            scale_ref[i, k:k + 1, :] = part[k, r:r + 1, end]
    ends_ref[0] = u_ext[late + 1, :, end]
    for side in range(sides):
        piece_copy(side, 1).wait_recv()
        ends_ref[1 + side] = v_ext[side, late + 1, :, end]

    for side in range(sides):
        pltpu.make_async_copy(raw, raw, field_send.at[side]).wait()
    for _, middle, turn, _, cross_copy, _ in hops:
        pl.when(middle | turn)(cross_copy.wait_send)

    @pl.when(sends_coup)
    def _():
        coup_copy.wait_send()
        if shared:
            coup_pass.wait_send()

    @pl.when(has_above)
    def _():
        strips(1 + sides, other_send.at[1]).wait()
        kx_copy.wait_send()

    @pl.when(has_below)
    def _():
        strips(1 + sides, other_send.at[2]).wait()


def shards(n_mode, n_space, field, kappa_x, kappa_y, coupling, pattern):
    mb, rows, ny = field.shape
    terms = kappa_x.shape[0]
    sides = 1 if n_mode == 2 else 2
    vmem = pl.BlockSpec(memory_space=pltpu.VMEM)
    hbm = pl.BlockSpec(memory_space=pltpu.HBM)
    across = rows * ny // 128
    width = min(LATE, ny - 512)
    results = pl.pallas_call(
        functools.partial(kernel, n_mode, n_space),
        out_shape=[
            jax.ShapeDtypeStruct((mb * across, 128), jnp.float32),
            jax.ShapeDtypeStruct((terms * mb, 4 * mb), jnp.bfloat16),
            jax.ShapeDtypeStruct((1 + sides, mb, width), jnp.bfloat16),
            jax.ShapeDtypeStruct((4, mb, 512), jnp.float32),
            jax.ShapeDtypeStruct((4, terms, width), jnp.float32),
        ],
        in_specs=[hbm] * 5,
        out_specs=[vmem] * 5,
        scratch_shapes=[
            pltpu.VMEM(field.shape, jnp.bfloat16),
            pltpu.VMEM((sides, mb, rows, min(EARLY, ny // 2)), jnp.bfloat16),
            pltpu.VMEM((mb * rows, 128), jnp.float32),
            pltpu.VMEM((rows + 2, mb, ny), jnp.bfloat16),
            pltpu.VMEM((sides, rows + 2, mb, ny), jnp.bfloat16),
            pltpu.VMEM((2,) + kappa_x.shape, jnp.float32),
            pltpu.VMEM(kappa_y.shape, jnp.float32),
            pltpu.VMEM(coupling.shape, jnp.bfloat16),
            pltpu.VMEM(pattern.shape, jnp.int32),
            pltpu.VMEM((terms * mb * mb // 128, 128), jnp.bfloat16),
            pltpu.VMEM((terms * mb * mb // 128, 128), jnp.bfloat16),
            pltpu.VMEM((1, mb, ny - min(EARLY, ny // 2)), jnp.bfloat16),
            pltpu.VMEM((terms * mb, 4 * mb), jnp.float32),
            pltpu.VMEM((terms * mb, 4 * mb), jnp.float32),
            pltpu.VMEM((terms, 8, ny), jnp.float32),
            pltpu.VMEM((mb, ny), jnp.float32),
            pltpu.VMEM((mb, ny), jnp.float32),
            pltpu.VMEM((mb, ny), jnp.float32),
            pltpu.VMEM((mb, ny), jnp.float32),
            pltpu.VMEM((mb, ny), jnp.float32),
            pltpu.VMEM((mb, ny), jnp.float32),
            pltpu.VMEM((mb, ny), jnp.float32),
            pltpu.SemaphoreType.DMA((4,)),
            pltpu.SemaphoreType.DMA((sides,)),
            pltpu.SemaphoreType.DMA((sides,)),
            pltpu.SemaphoreType.DMA((sides, rows // 2 + 1)),
            pltpu.SemaphoreType.DMA((sides, 2)),
            pltpu.SemaphoreType.DMA((5,)),
            pltpu.SemaphoreType.DMA((4,)),
            pltpu.SemaphoreType.DMA((2,)),
            pltpu.SemaphoreType.REGULAR,
        ],
        compiler_params=pltpu.CompilerParams(collective_id=0, has_side_effects=True, vmem_limit_bytes=24 * 2**20),
    )(*[pltpu.with_memory_space_constraint(x, pltpu.HBM)
        for x in (field, kappa_x, kappa_y, coupling, pattern)])
    handed = [results[0].reshape(mb, across, 128)] + list(results[1:])
    handed = [pltpu.with_memory_space_constraint(x, pltpu.VMEM) for x in handed]
    out = pl.pallas_call(
        functools.partial(closing, rows),
        out_shape=jax.ShapeDtypeStruct((mb, across, 128), jnp.float32),
        in_specs=[vmem] * 5,
        out_specs=hbm,
        scratch_shapes=[
            pltpu.VMEM((mb, (width + 128) // 16, 128), jnp.float32),
            pltpu.SemaphoreType.DMA((2,)),
        ],
        compiler_params=pltpu.CompilerParams(vmem_limit_bytes=8 * 2**20),
    )(*handed)
    tiles = out.reshape(mb, rows // 8, ny // 128, 8, 128)
    return jnp.swapaxes(tiles, 2, 3).reshape(mb, rows, ny)


def solution(mesh):
    placed = (
        P("mode", "space", None),
        P(None, "space", None),
        P(None, "space", None),
        P("mode", None, None, None),
        P("mode", None, None, None),
    )
    return jax.shard_map(
        functools.partial(shards, mesh.shape["mode"], mesh.shape["space"]),
        mesh=mesh, in_specs=placed, out_specs=P("mode", "space", None), check_vma=False)
```

```python
import functools

import jax
import jax.numpy as jnp
from jax import lax
from jax.experimental import pallas as pl
from jax.experimental.pallas import tpu as pltpu
from jax.sharding import PartitionSpec as P

LANES = 256
PART = 16
EARLY = 128
LATE = 384
ASIDE = 384


def weighted_sums(w, mb, terms, *weights):
    parts = [[] for _ in weights]
    scales = [[weight(k) for k in range(terms)] for weight in weights]
    for m in range(0, mb, PART):
        totals = [None] * len(weights)
        for k in range(terms):
            part = w[m * terms + k * PART:m * terms + (k + 1) * PART]
            for i in range(len(weights)):
                value = scales[i][k] * part
                totals[i] = value if totals[i] is None else totals[i] + value
        for i in range(len(weights)):
            parts[i].append(totals[i])
    return [jnp.concatenate(p, axis=0) for p in parts]


def from_left(q):
    lane = lax.broadcasted_iota(jnp.int32, q.shape, 1)
    return jnp.where(lane == 0, 0.0, pltpu.roll(q, 1, axis=1))


def from_right(z):
    lane = lax.broadcasted_iota(jnp.int32, z.shape, 1)
    return jnp.where(lane == z.shape[1] - 1, 0.0, pltpu.roll(z, z.shape[1] - 1, axis=1))


def closing(rows, x_ref, coef_ref, ends_ref, rim_ref, scale_ref, out_ref, tail, sem):
    mb = ends_ref.shape[1]
    sides = ends_ref.shape[0] - 1
    terms, width = scale_ref.shape[1:]
    done = pl.ds(0, x_ref.shape[1] - tail.shape[1])
    left_over = pl.ds(x_ref.shape[1] - tail.shape[1], tail.shape[1])
    bulk = pltpu.make_async_copy(x_ref.at[:, done], out_ref.at[:, done], sem.at[0])
    bulk.start()
    tail[...] = x_ref[:, left_over]
    flat = tail.reshape(mb * tail.shape[1], 128)

    def put(r, first, value):
        for at in range(0, value.shape[1], 128):
            flat[pl.ds((first + at) // 16 + r % 8, mb, stride=tail.shape[1]), :] = value[:, at:at + 128]

    u, vs = ends_ref[0], [ends_ref[1 + side] for side in range(sides)]
    w = jnp.dot(coef_ref[...], jnp.concatenate([u, u, vs[0], vs[-1]], axis=0), preferred_element_type=jnp.float32)
    a, b, q, z = weighted_sums(w, mb, terms, *[lambda k, i=i: scale_ref[i, k:k + 1, :] for i in range(4)])
    put(rows - 3, 128, rim_ref[0, :, :width] - a)
    put(rows - 1, 128, rim_ref[1, :, :width] - b)
    total = jnp.concatenate([rim_ref[3, :, :128], a + b + q + z - rim_ref[2, :, :width]], axis=1)
    left = pltpu.roll(jnp.concatenate([rim_ref[3, :, 256:512], q], axis=1), 1, axis=1)[:, 128:]
    right = from_right(jnp.concatenate([rim_ref[3, :, 128:256], z], axis=1))
    put(rows - 2, 0, total - left - right)
    rest = pltpu.make_async_copy(tail, out_ref.at[:, left_over], sem.at[1])
    rest.start()
    bulk.wait()
    rest.wait()


def kernel(n_mode, n_space, field_hbm, kx_hbm, ky_hbm, coup_hbm, pat_hbm, out_ref, coef_ref, ends_ref, rim_ref, scale_ref,
           raw, raw_in, tall, u_ext, v_ext, kappa, ky_left, coup, pat, packed, packed_in, relay, own_ref, mixed_ref,
           kx_in, pend, low, q_row, z_row, first_row, last_row, high,
           local_sem, field_send, early_recv, row_recv, piece_recv, other_send, other_recv, relay_sem, hello):
    mb, rows, ny = field_hbm.shape
    group = 128 // mb
    terms = kx_hbm.shape[0]
    sides = v_ext.shape[0]
    early = raw_in.shape[-1]
    mode = lax.axis_index("mode")
    space = lax.axis_index("space")
    above = {"space": lax.rem(space + 1, n_space)}
    below = {"space": lax.rem(space + n_space - 1, n_space)}
    upper = {"mode": lax.rem(mode + 1, n_mode)}
    lower = {"mode": lax.rem(mode + n_mode - 1, n_mode)}
    has_below = space > 0
    has_above = space < n_space - 1
    kx_ref, ky_ref = kappa.at[0], kappa.at[1]

    barrier = pltpu.get_barrier_semaphore()

    def greet(target):
        pl.semaphore_signal(barrier, inc=1, device_id=target, device_id_type=pl.DeviceIdType.MESH)

    for target in (upper, lower)[:sides]:
        greet(target)
    odd = lax.rem(space, 2) == 1
    pl.when(odd)(lambda: greet(below))
    pl.when(odd & has_above)(lambda: greet(above))
    neighbours = jnp.where(has_below, 1, 0) + jnp.where(has_above, 1, 0)

    field_load = pltpu.make_async_copy(field_hbm, raw, local_sem.at[0])
    coup_load = pltpu.make_async_copy(coup_hbm, coup, local_sem.at[1])
    pat_load = pltpu.make_async_copy(pat_hbm, pat, local_sem.at[2])
    kx_load = pltpu.make_async_copy(kx_hbm, kx_ref, local_sem.at[3])
    ky_load = pltpu.make_async_copy(ky_hbm, ky_ref, local_sem.at[3])
    for copy in (field_load, coup_load, pat_load, kx_load, ky_load):
        copy.start()

    def masked(slot, k):
        return jnp.where(pat[slot, k] > 0, coup[slot, k].astype(jnp.float32), 0.0)

    def placed(block, shape, offset, flip=False):
        spot = lax.broadcasted_iota(jnp.int32, shape, 0) + offset
        place = jnp.where(lax.broadcasted_iota(jnp.int32, shape, 1) == spot, 1.0, 0.0).astype(jnp.bfloat16)
        return lax.dot_general(block.astype(jnp.bfloat16), place, (((0 if flip else 1,), (0,)), ((), ())),
                               preferred_element_type=jnp.float32)

    def by_rows(source, target, first, count, width):
        for c in range(0, width, 128):
            tall[:mb * count] = source[:, first:first + count, c:c + 128].astype(jnp.float32).reshape(mb * count, 128)
            for r in range(count):
                target[first + r + 1, :, c:c + 128] = tall[pl.ds(r, mb, stride=count), :].astype(jnp.bfloat16)

    pl.semaphore_wait(barrier, sides + jnp.where(odd, 0, neighbours))

    def answer(target):
        pl.semaphore_signal(hello, inc=1, device_id=target, device_id_type=pl.DeviceIdType.MESH)

    def remote(src, dst, send, recv, target):
        return pltpu.make_async_remote_copy(
            src_ref=src, dst_ref=dst, send_sem=send, recv_sem=recv,
            device_id=target, device_id_type=pl.DeviceIdType.MESH)

    towards = (lower, upper)
    split = ny - ends_ref.shape[-1]
    pieces = [(early, split), (split, ny)]
    pairs = (rows - 6) // 2
    rest = pl.ds(early, ny - early)

    def rows_copy(side, first, count, at, cols=rest, recv=row_recv):
        part = pl.ds(first + 1, count)
        return remote(u_ext.at[part, :, cols], v_ext.at[side, part, :, cols],
                      field_send.at[side], recv.at[side, at], towards[side])

    def pair_copy(side, h):
        return rows_copy(side, 2 * h + 3, 2, h + 4)

    def early_row(side):
        return rows_copy(side, 2, 1, 2)

    def late_row(side):
        return rows_copy(side, rows - 3, 1, 3)

    def piece_copy(side, p):
        first, last = pieces[p]
        return rows_copy(side, rows - 2, 1, p, pl.ds(first, last - first), piece_recv)

    def early_copy(side):
        return remote(field_hbm.at[:, :, pl.ds(0, early)], raw_in.at[side], field_send.at[side], early_recv.at[side], towards[side])

    def halo_up(side):
        return remote(v_ext.at[side, rows], v_ext.at[side, 0], other_send.at[1], other_recv.at[1], above)

    def halo_down(side):
        return remote(v_ext.at[side, 1], v_ext.at[side, rows + 1], other_send.at[2], other_recv.at[2], below)

    shared = n_space % 2 == 0
    sends_coup = lax.rem(space, 2) == 0 if shared else space >= 0
    coup_pass = remote(packed_in, packed_in, other_send.at[3], other_recv.at[0], above)
    coup_copy = remote(packed, packed_in, other_send.at[0], other_recv.at[0], upper)
    last_copy = remote(u_ext.at[rows], u_ext.at[0], other_send.at[1], other_recv.at[1], above)
    first_copy = remote(u_ext.at[1], u_ext.at[rows + 1], other_send.at[2], other_recv.at[2], below)
    kx_copy = remote(kx_hbm.at[:, pl.ds(rows - 8, 8), :], kx_in, other_send.at[1], other_recv.at[1], above)
    upward = 1 + sides + terms * 16 // mb

    def strips(count, sem):
        part = u_ext.at[pl.ds(0, count)]
        return pltpu.make_async_copy(part, part, sem)

    for side in range(sides):
        early_copy(side).start()
    pl.when(jnp.logical_not(odd) & has_below)(lambda: answer(below))
    pl.when(jnp.logical_not(odd) & has_above)(lambda: answer(above))

    coup_load.wait()
    pat_load.wait()

    @pl.when(sends_coup)
    def _():
        for q in range(terms // group):
            beside = None
            for p in range(group):
                part = placed(masked(1, q * group + p), (mb, 128), p * mb, flip=True)
                beside = part if beside is None else beside + part
            packed[q * mb:(q + 1) * mb] = beside.astype(jnp.bfloat16)
        coup_copy.start()

    field_load.wait()
    by_rows(raw, u_ext, 0, rows, ny)
    pl.when(odd)(lambda: pl.semaphore_wait(hello, neighbours))

    detours = [(1, ny - early), (3, min(ASIDE, ny - early))] if sides == 1 and n_space > 4 else []
    weak = odd
    yields = weak if detours else space < 0
    late_yield = odd & (mode == 0) if detours else space < 0
    hops = []
    for at, width in detours:
        part = pl.ds(early, width)
        held_part = relay.at[:, :, pl.ds(0, width)]
        hops.append((
            (mode == 1) & (space == at), (mode == 1) & (space == at + 1), (mode == 0) & (space == at + 1),
            remote(u_ext.at[pl.ds(3, 1), :, part], held_part, field_send.at[0], relay_sem.at[0], above),
            remote(held_part, held_part, relay_sem.at[1], relay_sem.at[0], upper),
            remote(held_part, v_ext.at[0, pl.ds(3, 1), :, part], relay_sem.at[1], row_recv.at[0, 2], below)))

    def early_rows(here):
        whole = here
        for (at, width), hop in zip(detours, hops):
            whole = whole & jnp.logical_not(hop[0])
            if width < ny - early:
                pl.when(here & hop[0])(rows_copy(0, 2, 1, 2, pl.ds(early + width, ny - early - width)).start)
        for side in range(sides):
            pl.when(whole)(early_row(side).start)

    for source, _, _, leave_copy, _, _ in hops:
        pl.when(source)(leave_copy.start)
    for side in range(sides):
        rows_copy(side, 0, 2, 0).start()
    pl.when(has_below)(first_copy.start)
    for _, middle, _, leave_copy, cross_copy, _ in hops:
        @pl.when(middle)
        def _():
            leave_copy.wait_recv()
            cross_copy.start()
    for side in range(sides):
        rows_copy(side, rows - 1, 1, 1).start()
    early_rows(jnp.logical_not(late_yield))
    turns = space < 0
    for hop in hops:
        turns = turns | hop[2]

    if detours:
        pl.when(turns)(pair_copy(0, 0).start)

    def send_rest():
        if detours:
            early_rows(late_yield)
        for side in range(sides):
            @pl.loop(jnp.where(turns, 1, 0), pairs)
            def _(h):
                pair_copy(side, h).start()
        for side in range(sides):
            late_row(side).start()
        for p in range(len(pieces)):
            for side in range(sides):
                piece_copy(side, p).start()

        @pl.when(has_above)
        def _():
            last_copy.start()
            kx_copy.start()

    pl.when(jnp.logical_not(yields | turns))(send_rest)

    for k in range(terms):
        half = masked(0, k) * 0.5
        shape = (mb, 4 * mb)
        coef = placed(half, shape, 0) + placed(half, shape, mb, flip=True) + placed(masked(1, k), shape, 2 * mb)
        own_ref[k * mb:(k + 1) * mb] = coef

    for side in range(sides):
        early_copy(side).wait_recv()
    for side in range(sides):
        by_rows(raw_in.at[side], v_ext.at[side], 0, rows, early)
    coup_copy.wait_recv()
    if shared:
        pl.when(sends_coup)(coup_pass.start)
    pltpu.make_async_copy(kappa, kappa, local_sem.at[3]).wait()
    for k in range(terms):
        lane = lax.broadcasted_iota(jnp.int32, (rows, ny), 1)
        ky_left[k] = jnp.where(lane == 0, 0.0, pltpu.roll(ky_ref[k], 1, axis=1))
    for k in range(terms):
        q, p = divmod(k, group)
        shape = (mb, 4 * mb)
        coef = (own_ref[k * mb:(k + 1) * mb]
                + placed(packed_in[q * mb:(q + 1) * mb, p * mb:(p + 1) * mb], shape, 3 * mb))
        for m in range(0, mb, PART):
            own_at = m * terms + k * PART
            mixed_ref[own_at:own_at + PART] = coef[m:m + PART]
    coef_ref[...] = mixed_ref[...].astype(jnp.bfloat16)
    for side in range(sides):
        rows_copy(side, 0, 2, 0).wait_recv()
        pl.when(has_below)(halo_down(side).start)
    for _, _, turn, _, cross_copy, come_copy in hops:
        @pl.when(turn)
        def _():
            cross_copy.wait_recv()
            come_copy.start()
    if detours:
        pl.when(yields | turns)(send_rest)
    for side in range(sides):
        rows_copy(side, rows - 1, 1, 1).wait_recv()
        pl.when(has_above)(halo_up(side).start)

    coef = coef_ref[...]
    final = rows - 1
    late = rows - 2

    def w_of(e, cols):
        u = u_ext[e, :, cols]
        vs = [v_ext[side, e, :, cols] for side in range(sides)]
        return jnp.dot(coef, jnp.concatenate([u, u, vs[0], vs[-1]], axis=0), preferred_element_type=jnp.float32)

    def sums(w, *weights):
        return weighted_sums(w, mb, terms, *weights)

    def row_of(ref, r, cols):
        return lambda k: ref[k, pl.ds(r, 1), cols]

    blocks = [pl.ds(c, LANES) for c in range(0, ny, LANES)]

    def put(r, cols, value):
        for at in range(0, cols.size, 128):
            tile = (cols.start + at) // 128
            start = (r // 8) * 8 * (ny // 128) + tile * 8 + r % 8
            out_ref[pl.ds(start, mb, stride=rows * (ny // 128)), :] = value[:, at:at + 128]

    def row_step(r, give):
        for cols in blocks:
            a, b, q, z = sums(w_of(r + 1, cols), row_of(kx_ref, r - 1, cols), row_of(kx_ref, r, cols),
                              row_of(ky_ref, r, cols), row_of(ky_left, r, cols))
            give(cols, a)
            pend[:, cols] = a + b + q + z - low[:, cols]
            low[:, cols] = b
            q_row[:, cols] = q
            z_row[:, cols] = z
        pend[...] = pend[...] - from_left(q_row[...]) - from_right(z_row[...])

    def full_step(r):
        row_step(r, lambda cols, a: put(r - 1, cols, pend[:, cols] - a))

    def edges():
        @pl.when(has_below)
        def _():
            strips(upward, other_recv.at[1]).wait()

        @pl.when(has_above)
        def _():
            strips(1 + sides, other_recv.at[2]).wait()

        def blank(e):
            u_ext[e] = jnp.zeros((mb, ny), jnp.bfloat16)
            for side in range(sides):
                v_ext[side, e] = jnp.zeros((mb, ny), jnp.bfloat16)

        @pl.when(jnp.logical_not(has_below))
        def _():
            blank(0)
            kx_in[...] = jnp.zeros_like(kx_in)

        @pl.when(jnp.logical_not(has_above))
        def _():
            blank(rows + 1)

        for cols in blocks:
            outer = lambda k: kx_in[k, 7:8, cols]
            put(0, cols, first_row[:, cols] + sums(w_of(1, cols), outer)[0] - sums(w_of(0, cols), outer)[0])
            a, b, q, z = sums(w_of(rows, cols), row_of(kx_ref, late, cols), row_of(kx_ref, final, cols),
                              row_of(ky_ref, final, cols), row_of(ky_left, final, cols))
            last_row[:, cols] = a + b + q + z - sums(w_of(rows + 1, cols), row_of(kx_ref, final, cols))[0]
            high[:, cols] = a
            first_row[:, cols] = q
            z_row[:, cols] = z
        last_row[...] = last_row[...] - from_left(first_row[...]) - from_right(z_row[...])

    for cols in blocks:
        b, q, z = sums(w_of(1, cols), row_of(kx_ref, 0, cols), row_of(ky_ref, 0, cols), row_of(ky_left, 0, cols))
        low[:, cols] = b
        first_row[:, cols] = b + q + z
        q_row[:, cols] = q
        z_row[:, cols] = z
    first_row[...] = first_row[...] - from_left(q_row[...]) - from_right(z_row[...])

    def take_first(cols, a):
        first_row[:, cols] = first_row[:, cols] - a

    row_step(1, take_first)

    for side in range(sides):
        early_row(side).wait_recv()
    full_step(2)

    @pl.loop(0, pairs)
    def _(h):
        pl.when(h == pairs // 2)(edges)
        for side in range(sides):
            pair_copy(side, h).wait_recv()
        full_step(2 * h + 3)
        full_step(2 * h + 4)

    for side in range(sides):
        late_row(side).wait_recv()
    full_step(rows - 3)

    high[...] = high[...] + low[...]

    last = pieces[0][1]
    cols = pl.ds(0, last)
    for side in range(sides):
        piece_copy(side, 0).wait_recv()
    a, b, q, z = sums(w_of(late + 1, cols), row_of(kx_ref, late - 1, cols), row_of(kx_ref, late, cols),
                      row_of(ky_ref, late, cols), row_of(ky_left, late, cols))
    put(late - 1, cols, pend[:, cols] - a)
    put(final, cols, last_row[:, cols] - b)
    total = a + b + q + z - high[:, cols]
    right = pltpu.roll(z, last - 1, axis=1)
    put(late, pl.ds(0, last - 128), (total - from_left(q) - right)[:, :last - 128])
    rim_ref[3, :, :128] = total[:, last - 128:]
    rim_ref[3, :, 128:256] = z[:, last - 128:]
    rim_ref[3, :, 256:512] = q[:, last - 256:]
    end = pl.ds(last, ny - last)
    for i, part in enumerate((pend, last_row, high)):
        rim_ref[i, :, :ny - last] = part[:, end]
    for k in range(terms):
        for i, (part, r) in enumerate(((kx_ref, late - 1), (kx_ref, late), (ky_ref, late), (ky_left, late))):
            scale_ref[i, k:k + 1, :] = part[k, r:r + 1, end]
    ends_ref[0] = u_ext[late + 1, :, end]
    for side in range(sides):
        piece_copy(side, 1).wait_recv()
        ends_ref[1 + side] = v_ext[side, late + 1, :, end]

    for side in range(sides):
        pltpu.make_async_copy(raw, raw, field_send.at[side]).wait()
    for _, middle, turn, _, cross_copy, _ in hops:
        pl.when(middle | turn)(cross_copy.wait_send)

    @pl.when(sends_coup)
    def _():
        coup_copy.wait_send()
        if shared:
            coup_pass.wait_send()

    @pl.when(has_above)
    def _():
        strips(upward, other_send.at[1]).wait()

    @pl.when(has_below)
    def _():
        strips(1 + sides, other_send.at[2]).wait()


def shards(n_mode, n_space, field, kappa_x, kappa_y, coupling, pattern):
    mb, rows, ny = field.shape
    terms = kappa_x.shape[0]
    sides = 1 if n_mode == 2 else 2
    vmem = pl.BlockSpec(memory_space=pltpu.VMEM)
    hbm = pl.BlockSpec(memory_space=pltpu.HBM)
    across = rows * ny // 128
    width = min(LATE, ny - 512)
    results = pl.pallas_call(
        functools.partial(kernel, n_mode, n_space),
        out_shape=[
            jax.ShapeDtypeStruct((mb * across, 128), jnp.float32),
            jax.ShapeDtypeStruct((terms * mb, 4 * mb), jnp.bfloat16),
            jax.ShapeDtypeStruct((1 + sides, mb, width), jnp.bfloat16),
            jax.ShapeDtypeStruct((4, mb, 512), jnp.float32),
            jax.ShapeDtypeStruct((4, terms, width), jnp.float32),
        ],
        in_specs=[hbm] * 5,
        out_specs=[vmem] * 5,
        scratch_shapes=[
            pltpu.VMEM(field.shape, jnp.bfloat16),
            pltpu.VMEM((sides, mb, rows, min(EARLY, ny // 2)), jnp.bfloat16),
            pltpu.VMEM((mb * rows, 128), jnp.float32),
            pltpu.VMEM((rows + 2, mb, ny), jnp.bfloat16),
            pltpu.VMEM((sides, rows + 2, mb, ny), jnp.bfloat16),
            pltpu.VMEM((2,) + kappa_x.shape, jnp.float32),
            pltpu.VMEM(kappa_y.shape, jnp.float32),
            pltpu.VMEM(coupling.shape, jnp.bfloat16),
            pltpu.VMEM(pattern.shape, jnp.int32),
            pltpu.VMEM((terms * mb * mb // 128, 128), jnp.bfloat16),
            pltpu.VMEM((terms * mb * mb // 128, 128), jnp.bfloat16),
            pltpu.VMEM((1, mb, ny - min(EARLY, ny // 2)), jnp.bfloat16),
            pltpu.VMEM((terms * mb, 4 * mb), jnp.float32),
            pltpu.VMEM((terms * mb, 4 * mb), jnp.float32),
            pltpu.VMEM((terms, 8, ny), jnp.float32),
            pltpu.VMEM((mb, ny), jnp.float32),
            pltpu.VMEM((mb, ny), jnp.float32),
            pltpu.VMEM((mb, ny), jnp.float32),
            pltpu.VMEM((mb, ny), jnp.float32),
            pltpu.VMEM((mb, ny), jnp.float32),
            pltpu.VMEM((mb, ny), jnp.float32),
            pltpu.VMEM((mb, ny), jnp.float32),
            pltpu.SemaphoreType.DMA((4,)),
            pltpu.SemaphoreType.DMA((sides,)),
            pltpu.SemaphoreType.DMA((sides,)),
            pltpu.SemaphoreType.DMA((sides, rows // 2 + 1)),
            pltpu.SemaphoreType.DMA((sides, 2)),
            pltpu.SemaphoreType.DMA((4,)),
            pltpu.SemaphoreType.DMA((3,)),
            pltpu.SemaphoreType.DMA((2,)),
            pltpu.SemaphoreType.REGULAR,
        ],
        compiler_params=pltpu.CompilerParams(collective_id=0, has_side_effects=True, vmem_limit_bytes=24 * 2**20),
    )(*[pltpu.with_memory_space_constraint(x, pltpu.HBM)
        for x in (field, kappa_x, kappa_y, coupling, pattern)])
    handed = [results[0].reshape(mb, across, 128)] + list(results[1:])
    handed = [pltpu.with_memory_space_constraint(x, pltpu.VMEM) for x in handed]
    out = pl.pallas_call(
        functools.partial(closing, rows),
        out_shape=jax.ShapeDtypeStruct((mb, across, 128), jnp.float32),
        in_specs=[vmem] * 5,
        out_specs=hbm,
        scratch_shapes=[
            pltpu.VMEM((mb, (width + 128) // 16, 128), jnp.float32),
            pltpu.SemaphoreType.DMA((2,)),
        ],
        compiler_params=pltpu.CompilerParams(vmem_limit_bytes=8 * 2**20),
    )(*handed)
    tiles = out.reshape(mb, rows // 8, ny // 128, 8, 128)
    return jnp.swapaxes(tiles, 2, 3).reshape(mb, rows, ny)


def solution(mesh):
    placed = (
        P("mode", "space", None),
        P(None, "space", None),
        P(None, "space", None),
        P("mode", None, None, None),
        P("mode", None, None, None),
    )
    return jax.shard_map(
        functools.partial(shards, mesh.shape["mode"], mesh.shape["space"]),
        mesh=mesh, in_specs=placed, out_specs=P("mode", "space", None), check_vma=False)
```

```python
import functools

import jax
import jax.numpy as jnp
from jax import lax
from jax.experimental import pallas as pl
from jax.experimental.pallas import tpu as pltpu
from jax.sharding import PartitionSpec as P

LANES = 256
PART = 16
EARLY = 128
LATE = 384
ASIDE = 384


def weighted_sums(w, mb, terms, *weights):
    parts = [[] for _ in weights]
    scales = [[weight(k) for k in range(terms)] for weight in weights]
    for m in range(0, mb, PART):
        totals = [None] * len(weights)
        for k in range(terms):
            part = w[m * terms + k * PART:m * terms + (k + 1) * PART]
            for i in range(len(weights)):
                value = scales[i][k] * part
                totals[i] = value if totals[i] is None else totals[i] + value
        for i in range(len(weights)):
            parts[i].append(totals[i])
    return [jnp.concatenate(p, axis=0) for p in parts]


def from_left(q):
    lane = lax.broadcasted_iota(jnp.int32, q.shape, 1)
    return jnp.where(lane == 0, 0.0, pltpu.roll(q, 1, axis=1))


def from_right(z):
    lane = lax.broadcasted_iota(jnp.int32, z.shape, 1)
    return jnp.where(lane == z.shape[1] - 1, 0.0, pltpu.roll(z, z.shape[1] - 1, axis=1))


def closing(rows, x_ref, coef_ref, ends_ref, rim_ref, scale_ref, out_ref, tail, sem):
    mb = ends_ref.shape[1]
    sides = ends_ref.shape[0] - 1
    terms, width = scale_ref.shape[1:]
    done = pl.ds(0, x_ref.shape[1] - tail.shape[1])
    left_over = pl.ds(x_ref.shape[1] - tail.shape[1], tail.shape[1])
    bulk = pltpu.make_async_copy(x_ref.at[:, done], out_ref.at[:, done], sem.at[0])
    bulk.start()
    tail[...] = x_ref[:, left_over]
    flat = tail.reshape(mb * tail.shape[1], 128)

    def put(r, first, value):
        for at in range(0, value.shape[1], 128):
            flat[pl.ds((first + at) // 16 + r % 8, mb, stride=tail.shape[1]), :] = value[:, at:at + 128]

    u, vs = ends_ref[0], [ends_ref[1 + side] for side in range(sides)]
    w = jnp.dot(coef_ref[...], jnp.concatenate([u, u, vs[0], vs[-1]], axis=0), preferred_element_type=jnp.float32)
    a, b, q, z = weighted_sums(w, mb, terms, *[lambda k, i=i: scale_ref[i, k:k + 1, :] for i in range(4)])
    put(rows - 3, 128, rim_ref[0, :, :width] - a)
    put(rows - 1, 128, rim_ref[1, :, :width] - b)
    total = jnp.concatenate([rim_ref[3, :, :128], a + b + q + z - rim_ref[2, :, :width]], axis=1)
    left = pltpu.roll(jnp.concatenate([rim_ref[3, :, 256:512], q], axis=1), 1, axis=1)[:, 128:]
    right = from_right(jnp.concatenate([rim_ref[3, :, 128:256], z], axis=1))
    put(rows - 2, 0, total - left - right)
    rest = pltpu.make_async_copy(tail, out_ref.at[:, left_over], sem.at[1])
    rest.start()
    bulk.wait()
    rest.wait()


def kernel(n_mode, n_space, field_hbm, kx_hbm, ky_hbm, coup_hbm, pat_hbm, out_ref, coef_ref, ends_ref, rim_ref, scale_ref,
           raw, raw_in, tall, u_ext, v_ext, kappa, ky_left, coup, pat, packed, packed_in, relay, own_ref, mixed_ref,
           kx_in, pend, low, q_row, z_row, first_row, last_row, high,
           local_sem, field_send, early_recv, row_recv, piece_recv, other_send, other_recv, relay_sem, hello):
    mb, rows, ny = field_hbm.shape
    group = 128 // mb
    terms = kx_hbm.shape[0]
    sides = v_ext.shape[0]
    early = raw_in.shape[-1]
    mode = lax.axis_index("mode")
    space = lax.axis_index("space")
    above = {"space": lax.rem(space + 1, n_space)}
    below = {"space": lax.rem(space + n_space - 1, n_space)}
    upper = {"mode": lax.rem(mode + 1, n_mode)}
    lower = {"mode": lax.rem(mode + n_mode - 1, n_mode)}
    has_below = space > 0
    has_above = space < n_space - 1
    kx_ref, ky_ref = kappa.at[0], kappa.at[1]

    barrier = pltpu.get_barrier_semaphore()

    def greet(target):
        pl.semaphore_signal(barrier, inc=1, device_id=target, device_id_type=pl.DeviceIdType.MESH)

    for target in (upper, lower)[:sides]:
        greet(target)
    odd = lax.rem(space, 2) == 1
    pl.when(odd)(lambda: greet(below))
    pl.when(odd & has_above)(lambda: greet(above))
    neighbours = jnp.where(has_below, 1, 0) + jnp.where(has_above, 1, 0)

    field_load = pltpu.make_async_copy(field_hbm, raw, local_sem.at[0])
    coup_load = pltpu.make_async_copy(coup_hbm, coup, local_sem.at[1])
    pat_load = pltpu.make_async_copy(pat_hbm, pat, local_sem.at[2])
    kx_load = pltpu.make_async_copy(kx_hbm, kx_ref, local_sem.at[3])
    ky_load = pltpu.make_async_copy(ky_hbm, ky_ref, local_sem.at[3])
    for copy in (field_load, coup_load, pat_load, kx_load, ky_load):
        copy.start()

    def masked(slot, k):
        return jnp.where(pat[slot, k] > 0, coup[slot, k].astype(jnp.float32), 0.0)

    def placed(block, shape, offset, flip=False):
        spot = lax.broadcasted_iota(jnp.int32, shape, 0) + offset
        place = jnp.where(lax.broadcasted_iota(jnp.int32, shape, 1) == spot, 1.0, 0.0).astype(jnp.bfloat16)
        return lax.dot_general(block.astype(jnp.bfloat16), place, (((0 if flip else 1,), (0,)), ((), ())),
                               preferred_element_type=jnp.float32)

    def by_rows(source, target, first, count, width):
        for c in range(0, width, 128):
            tall[:mb * count] = source[:, first:first + count, c:c + 128].astype(jnp.float32).reshape(mb * count, 128)
            for r in range(count):
                target[first + r + 1, :, c:c + 128] = tall[pl.ds(r, mb, stride=count), :].astype(jnp.bfloat16)

    pl.semaphore_wait(barrier, sides + jnp.where(odd, 0, neighbours))

    def answer(target):
        pl.semaphore_signal(hello, inc=1, device_id=target, device_id_type=pl.DeviceIdType.MESH)

    def remote(src, dst, send, recv, target):
        return pltpu.make_async_remote_copy(
            src_ref=src, dst_ref=dst, send_sem=send, recv_sem=recv,
            device_id=target, device_id_type=pl.DeviceIdType.MESH)

    towards = (lower, upper)
    split = ny - ends_ref.shape[-1]
    pieces = [(early, split), (split, ny)]
    pairs = (rows - 6) // 2
    rest = pl.ds(early, ny - early)

    def rows_copy(side, first, count, at, cols=rest, recv=row_recv):
        part = pl.ds(first + 1, count)
        return remote(u_ext.at[part, :, cols], v_ext.at[side, part, :, cols],
                      field_send.at[side], recv.at[side, at], towards[side])

    def pair_copy(side, h):
        return rows_copy(side, 2 * h + 3, 2, h + 4)

    def early_row(side):
        return rows_copy(side, 2, 1, 2)

    def late_row(side):
        return rows_copy(side, rows - 3, 1, 3)

    def piece_copy(side, p):
        first, last = pieces[p]
        return rows_copy(side, rows - 2, 1, p, pl.ds(first, last - first), piece_recv)

    def early_copy(side):
        return remote(field_hbm.at[:, :, pl.ds(0, early)], raw_in.at[side], field_send.at[side], early_recv.at[side], towards[side])

    def halo_up(side):
        return remote(v_ext.at[side, rows], v_ext.at[side, 0], other_send.at[1], other_recv.at[1], above)

    def halo_down(side):
        return remote(v_ext.at[side, 1], v_ext.at[side, rows + 1], other_send.at[2], other_recv.at[2], below)

    shared = n_space % 2 == 0
    sends_coup = lax.rem(space, 2) == 0 if shared else space >= 0
    coup_pass = remote(packed_in, packed_in, other_send.at[3], other_recv.at[0], above)
    coup_copy = remote(packed, packed_in, other_send.at[0], other_recv.at[0], upper)
    last_copy = remote(u_ext.at[rows], u_ext.at[0], other_send.at[1], other_recv.at[1], above)
    first_copy = remote(u_ext.at[1], u_ext.at[rows + 1], other_send.at[2], other_recv.at[2], below)
    kx_copy = remote(kx_hbm.at[:, pl.ds(rows - 8, 8), :], kx_in, other_send.at[1], other_recv.at[1], above)
    upward = 1 + sides + terms * 16 // mb

    def strips(count, sem):
        part = u_ext.at[pl.ds(0, count)]
        return pltpu.make_async_copy(part, part, sem)

    for side in range(sides):
        early_copy(side).start()
    pl.when(jnp.logical_not(odd) & has_below)(lambda: answer(below))
    pl.when(jnp.logical_not(odd) & has_above)(lambda: answer(above))

    coup_load.wait()
    pat_load.wait()

    @pl.when(sends_coup)
    def _():
        for q in range(terms // group):
            beside = None
            for p in range(group):
                part = placed(masked(1, q * group + p), (mb, 128), p * mb, flip=True)
                beside = part if beside is None else beside + part
            packed[q * mb:(q + 1) * mb] = beside.astype(jnp.bfloat16)
        coup_copy.start()

    field_load.wait()
    by_rows(raw, u_ext, 0, rows, ny)
    pl.when(odd)(lambda: pl.semaphore_wait(hello, neighbours))

    detours = [(1, ny - early), (3, min(ASIDE, ny - early))] if sides == 1 and n_space > 4 else []
    weak = odd
    yields = weak if detours else space < 0
    late_yield = odd & (mode == 0) if detours else space < 0
    hops = []
    for at, width in detours:
        part = pl.ds(early, width)
        held_part = relay.at[:, :, pl.ds(0, width)]
        hops.append((
            (mode == 1) & (space == at), (mode == 1) & (space == at + 1), (mode == 0) & (space == at + 1),
            remote(u_ext.at[pl.ds(3, 1), :, part], held_part, field_send.at[0], relay_sem.at[0], above),
            remote(held_part, held_part, relay_sem.at[1], relay_sem.at[0], upper),
            remote(held_part, v_ext.at[0, pl.ds(3, 1), :, part], relay_sem.at[1], row_recv.at[0, 2], below)))

    def early_rows(here):
        whole = here
        for (at, width), hop in zip(detours, hops):
            whole = whole & jnp.logical_not(hop[0])
            if width < ny - early:
                pl.when(here & hop[0])(rows_copy(0, 2, 1, 2, pl.ds(early + width, ny - early - width)).start)
        for side in range(sides):
            pl.when(whole)(early_row(side).start)

    for source, _, _, leave_copy, _, _ in hops:
        pl.when(source)(leave_copy.start)
    for side in range(sides):
        rows_copy(side, 0, 2, 0).start()
    pl.when(has_below)(first_copy.start)
    for _, middle, _, leave_copy, cross_copy, _ in hops:
        @pl.when(middle)
        def _():
            leave_copy.wait_recv()
            cross_copy.start()
    for side in range(sides):
        rows_copy(side, rows - 1, 1, 1).start()
    early_rows(jnp.logical_not(late_yield))
    turns = space < 0
    for hop in hops:
        turns = turns | hop[2]

    first_source = hops[0][0] if hops else space < 0
    if detours:
        pl.when(turns)(pair_copy(0, 0).start)
        pl.when(first_source)(late_row(0).start)

    def send_rest():
        if detours:
            early_rows(late_yield)
        for side in range(sides):
            @pl.loop(jnp.where(turns, 1, 0), pairs)
            def _(h):
                pair_copy(side, h).start()
        for side in range(sides):
            pl.when(jnp.logical_not(first_source))(late_row(side).start)
        for p in range(len(pieces)):
            for side in range(sides):
                piece_copy(side, p).start()

        @pl.when(has_above)
        def _():
            last_copy.start()
            kx_copy.start()

    pl.when(jnp.logical_not(yields | turns))(send_rest)

    for k in range(terms):
        half = masked(0, k) * 0.5
        shape = (mb, 4 * mb)
        coef = placed(half, shape, 0) + placed(half, shape, mb, flip=True) + placed(masked(1, k), shape, 2 * mb)
        own_ref[k * mb:(k + 1) * mb] = coef

    for side in range(sides):
        early_copy(side).wait_recv()
    for side in range(sides):
        by_rows(raw_in.at[side], v_ext.at[side], 0, rows, early)
    coup_copy.wait_recv()
    if shared:
        pl.when(sends_coup)(coup_pass.start)
    pltpu.make_async_copy(kappa, kappa, local_sem.at[3]).wait()
    for k in range(terms):
        lane = lax.broadcasted_iota(jnp.int32, (rows, ny), 1)
        ky_left[k] = jnp.where(lane == 0, 0.0, pltpu.roll(ky_ref[k], 1, axis=1))
    for k in range(terms):
        q, p = divmod(k, group)
        shape = (mb, 4 * mb)
        coef = (own_ref[k * mb:(k + 1) * mb]
                + placed(packed_in[q * mb:(q + 1) * mb, p * mb:(p + 1) * mb], shape, 3 * mb))
        for m in range(0, mb, PART):
            own_at = m * terms + k * PART
            mixed_ref[own_at:own_at + PART] = coef[m:m + PART]
    coef_ref[...] = mixed_ref[...].astype(jnp.bfloat16)
    for side in range(sides):
        rows_copy(side, 0, 2, 0).wait_recv()
        pl.when(has_below)(halo_down(side).start)
    for _, _, turn, _, cross_copy, come_copy in hops:
        @pl.when(turn)
        def _():
            cross_copy.wait_recv()
            come_copy.start()
    if detours:
        pl.when(yields | turns)(send_rest)
    for side in range(sides):
        rows_copy(side, rows - 1, 1, 1).wait_recv()
        pl.when(has_above)(halo_up(side).start)

    coef = coef_ref[...]
    final = rows - 1
    late = rows - 2

    def w_of(e, cols):
        u = u_ext[e, :, cols]
        vs = [v_ext[side, e, :, cols] for side in range(sides)]
        return jnp.dot(coef, jnp.concatenate([u, u, vs[0], vs[-1]], axis=0), preferred_element_type=jnp.float32)

    def sums(w, *weights):
        return weighted_sums(w, mb, terms, *weights)

    def row_of(ref, r, cols):
        return lambda k: ref[k, pl.ds(r, 1), cols]

    blocks = [pl.ds(c, LANES) for c in range(0, ny, LANES)]

    def put(r, cols, value):
        for at in range(0, cols.size, 128):
            tile = (cols.start + at) // 128
            start = (r // 8) * 8 * (ny // 128) + tile * 8 + r % 8
            out_ref[pl.ds(start, mb, stride=rows * (ny // 128)), :] = value[:, at:at + 128]

    def row_step(r, give):
        for cols in blocks:
            a, b, q, z = sums(w_of(r + 1, cols), row_of(kx_ref, r - 1, cols), row_of(kx_ref, r, cols),
                              row_of(ky_ref, r, cols), row_of(ky_left, r, cols))
            give(cols, a)
            pend[:, cols] = a + b + q + z - low[:, cols]
            low[:, cols] = b
            q_row[:, cols] = q
            z_row[:, cols] = z
        pend[...] = pend[...] - from_left(q_row[...]) - from_right(z_row[...])

    def full_step(r):
        row_step(r, lambda cols, a: put(r - 1, cols, pend[:, cols] - a))

    def edges():
        @pl.when(has_below)
        def _():
            strips(upward, other_recv.at[1]).wait()

        @pl.when(has_above)
        def _():
            strips(1 + sides, other_recv.at[2]).wait()

        def blank(e):
            u_ext[e] = jnp.zeros((mb, ny), jnp.bfloat16)
            for side in range(sides):
                v_ext[side, e] = jnp.zeros((mb, ny), jnp.bfloat16)

        @pl.when(jnp.logical_not(has_below))
        def _():
            blank(0)
            kx_in[...] = jnp.zeros_like(kx_in)

        @pl.when(jnp.logical_not(has_above))
        def _():
            blank(rows + 1)

        for cols in blocks:
            outer = lambda k: kx_in[k, 7:8, cols]
            put(0, cols, first_row[:, cols] + sums(w_of(1, cols), outer)[0] - sums(w_of(0, cols), outer)[0])
            a, b, q, z = sums(w_of(rows, cols), row_of(kx_ref, late, cols), row_of(kx_ref, final, cols),
                              row_of(ky_ref, final, cols), row_of(ky_left, final, cols))
            last_row[:, cols] = a + b + q + z - sums(w_of(rows + 1, cols), row_of(kx_ref, final, cols))[0]
            high[:, cols] = a
            first_row[:, cols] = q
            z_row[:, cols] = z
        last_row[...] = last_row[...] - from_left(first_row[...]) - from_right(z_row[...])

    for cols in blocks:
        b, q, z = sums(w_of(1, cols), row_of(kx_ref, 0, cols), row_of(ky_ref, 0, cols), row_of(ky_left, 0, cols))
        low[:, cols] = b
        first_row[:, cols] = b + q + z
        q_row[:, cols] = q
        z_row[:, cols] = z
    first_row[...] = first_row[...] - from_left(q_row[...]) - from_right(z_row[...])

    def take_first(cols, a):
        first_row[:, cols] = first_row[:, cols] - a

    row_step(1, take_first)

    for side in range(sides):
        early_row(side).wait_recv()
    full_step(2)

    @pl.loop(0, pairs)
    def _(h):
        pl.when(h == pairs // 2)(edges)
        for side in range(sides):
            pair_copy(side, h).wait_recv()
        full_step(2 * h + 3)
        full_step(2 * h + 4)

    for side in range(sides):
        late_row(side).wait_recv()
    full_step(rows - 3)

    high[...] = high[...] + low[...]

    last = pieces[0][1]
    cols = pl.ds(0, last)
    for side in range(sides):
        piece_copy(side, 0).wait_recv()
    a, b, q, z = sums(w_of(late + 1, cols), row_of(kx_ref, late - 1, cols), row_of(kx_ref, late, cols),
                      row_of(ky_ref, late, cols), row_of(ky_left, late, cols))
    put(late - 1, cols, pend[:, cols] - a)
    put(final, cols, last_row[:, cols] - b)
    total = a + b + q + z - high[:, cols]
    right = pltpu.roll(z, last - 1, axis=1)
    put(late, pl.ds(0, last - 128), (total - from_left(q) - right)[:, :last - 128])
    rim_ref[3, :, :128] = total[:, last - 128:]
    rim_ref[3, :, 128:256] = z[:, last - 128:]
    rim_ref[3, :, 256:512] = q[:, last - 256:]
    end = pl.ds(last, ny - last)
    for i, part in enumerate((pend, last_row, high)):
        rim_ref[i, :, :ny - last] = part[:, end]
    for k in range(terms):
        for i, (part, r) in enumerate(((kx_ref, late - 1), (kx_ref, late), (ky_ref, late), (ky_left, late))):
            scale_ref[i, k:k + 1, :] = part[k, r:r + 1, end]
    ends_ref[0] = u_ext[late + 1, :, end]
    for side in range(sides):
        piece_copy(side, 1).wait_recv()
        ends_ref[1 + side] = v_ext[side, late + 1, :, end]

    for side in range(sides):
        pltpu.make_async_copy(raw, raw, field_send.at[side]).wait()
    for _, middle, turn, _, cross_copy, _ in hops:
        pl.when(middle | turn)(cross_copy.wait_send)

    @pl.when(sends_coup)
    def _():
        coup_copy.wait_send()
        if shared:
            coup_pass.wait_send()

    @pl.when(has_above)
    def _():
        strips(upward, other_send.at[1]).wait()

    @pl.when(has_below)
    def _():
        strips(1 + sides, other_send.at[2]).wait()


def shards(n_mode, n_space, field, kappa_x, kappa_y, coupling, pattern):
    mb, rows, ny = field.shape
    terms = kappa_x.shape[0]
    sides = 1 if n_mode == 2 else 2
    vmem = pl.BlockSpec(memory_space=pltpu.VMEM)
    hbm = pl.BlockSpec(memory_space=pltpu.HBM)
    across = rows * ny // 128
    width = min(LATE, ny - 512)
    results = pl.pallas_call(
        functools.partial(kernel, n_mode, n_space),
        out_shape=[
            jax.ShapeDtypeStruct((mb * across, 128), jnp.float32),
            jax.ShapeDtypeStruct((terms * mb, 4 * mb), jnp.bfloat16),
            jax.ShapeDtypeStruct((1 + sides, mb, width), jnp.bfloat16),
            jax.ShapeDtypeStruct((4, mb, 512), jnp.float32),
            jax.ShapeDtypeStruct((4, terms, width), jnp.float32),
        ],
        in_specs=[hbm] * 5,
        out_specs=[vmem] * 5,
        scratch_shapes=[
            pltpu.VMEM(field.shape, jnp.bfloat16),
            pltpu.VMEM((sides, mb, rows, min(EARLY, ny // 2)), jnp.bfloat16),
            pltpu.VMEM((mb * rows, 128), jnp.float32),
            pltpu.VMEM((rows + 2, mb, ny), jnp.bfloat16),
            pltpu.VMEM((sides, rows + 2, mb, ny), jnp.bfloat16),
            pltpu.VMEM((2,) + kappa_x.shape, jnp.float32),
            pltpu.VMEM(kappa_y.shape, jnp.float32),
            pltpu.VMEM(coupling.shape, jnp.bfloat16),
            pltpu.VMEM(pattern.shape, jnp.int32),
            pltpu.VMEM((terms * mb * mb // 128, 128), jnp.bfloat16),
            pltpu.VMEM((terms * mb * mb // 128, 128), jnp.bfloat16),
            pltpu.VMEM((1, mb, ny - min(EARLY, ny // 2)), jnp.bfloat16),
            pltpu.VMEM((terms * mb, 4 * mb), jnp.float32),
            pltpu.VMEM((terms * mb, 4 * mb), jnp.float32),
            pltpu.VMEM((terms, 8, ny), jnp.float32),
            pltpu.VMEM((mb, ny), jnp.float32),
            pltpu.VMEM((mb, ny), jnp.float32),
            pltpu.VMEM((mb, ny), jnp.float32),
            pltpu.VMEM((mb, ny), jnp.float32),
            pltpu.VMEM((mb, ny), jnp.float32),
            pltpu.VMEM((mb, ny), jnp.float32),
            pltpu.VMEM((mb, ny), jnp.float32),
            pltpu.SemaphoreType.DMA((4,)),
            pltpu.SemaphoreType.DMA((sides,)),
            pltpu.SemaphoreType.DMA((sides,)),
            pltpu.SemaphoreType.DMA((sides, rows // 2 + 1)),
            pltpu.SemaphoreType.DMA((sides, 2)),
            pltpu.SemaphoreType.DMA((4,)),
            pltpu.SemaphoreType.DMA((3,)),
            pltpu.SemaphoreType.DMA((2,)),
            pltpu.SemaphoreType.REGULAR,
        ],
        compiler_params=pltpu.CompilerParams(collective_id=0, has_side_effects=True, vmem_limit_bytes=24 * 2**20),
    )(*[pltpu.with_memory_space_constraint(x, pltpu.HBM)
        for x in (field, kappa_x, kappa_y, coupling, pattern)])
    handed = [results[0].reshape(mb, across, 128)] + list(results[1:])
    handed = [pltpu.with_memory_space_constraint(x, pltpu.VMEM) for x in handed]
    out = pl.pallas_call(
        functools.partial(closing, rows),
        out_shape=jax.ShapeDtypeStruct((mb, across, 128), jnp.float32),
        in_specs=[vmem] * 5,
        out_specs=hbm,
        scratch_shapes=[
            pltpu.VMEM((mb, (width + 128) // 16, 128), jnp.float32),
            pltpu.SemaphoreType.DMA((2,)),
        ],
        compiler_params=pltpu.CompilerParams(vmem_limit_bytes=8 * 2**20),
    )(*handed)
    tiles = out.reshape(mb, rows // 8, ny // 128, 8, 128)
    return jnp.swapaxes(tiles, 2, 3).reshape(mb, rows, ny)


def solution(mesh):
    placed = (
        P("mode", "space", None),
        P(None, "space", None),
        P(None, "space", None),
        P("mode", None, None, None),
        P("mode", None, None, None),
    )
    return jax.shard_map(
        functools.partial(shards, mesh.shape["mode"], mesh.shape["space"]),
        mesh=mesh, in_specs=placed, out_specs=P("mode", "space", None), check_vma=False)
```
